256 devices in a mesh: gx: 4 (over x), gy: 8 (over z), gz: 8 (over y, core).
Axes of the slice: x: 4, y: 4, z: 8, core: 2. Of those that a mesh axis runs over, the one named last changes fastest.
Arguments:
- src_fields: float32 [8192, 1080], P(('gx', 'gy', 'gz')), may hold values from -6 to 6
- owner_peer: int32 [8192, 8, 1], P(('gx', 'gy', 'gz')), may hold values from 0 to 31; in each aligned block of 256 rows (0 to 255, 256 to 511, ..., all dimensions but the last counted through in order) at most 9 rows name the same one
- src_local: int32 [8192, 8], P(('gx', 'gy', 'gz')), may hold values from 0 to 31
- jac: float32 [8192, 4096], P(('gx', 'gy', 'gz')), may hold values from 0.25 to 4
Outputs:
- remapped: float32 [8192, 1080], P(('gx', 'gy', 'gz'))
- nodal_accel: float32 [8192, 648], P(('gx', 'gy', 'gz'))
The draws below stay inside these ranges and needn't reach their ends.
Inputs may be any that keep to these rules, and one draw needn't show every extreme that they name: owner_peer[r, k, 0] is the index, within the 32 devices that share target r's gz index (gx-major), of the device owning intersection k's source element; among the 256 intersections of one device's targets at most 9 name the same device, and some device reaches 9 in every draw.
All inputs are finite; a program needn't handle non-finite values.
Results may differ from the reference program's by a relative error of at most 0.0002.
Values sent between devices are 32-bit elements; how exact they have to be, the bound alone decides.
A program may use at most 64 MiB of HBM per device.

```python
import math
import jax
import jax.numpy as jnp
import numpy as np
from jax import lax

EX = 4
EY = 4
EZ = 2
FIELDS = 5
NB = 216
QP = 512
OVL = 8
E_DEV = 32
GROUP = 32
CAP = 9
ELEMS = 8192
N_GX = 4
N_GY = 8
N_GZ = 8


def touch_ends(entries, stream_key, low, top_value):
    spot = [jax.random.randint(jax.random.fold_in(stream_key, axis), (), 0, length) for axis, length in enumerate(entries.shape)]
    longest = entries.shape.index(max(entries.shape))
    next_to = spot[:longest] + [(spot[longest] + 1) % entries.shape[longest]] + spot[longest + 1:]
    return entries.at[tuple(spot)].set(low).at[tuple(next_to)].set(top_value)


def levels(rng, shape, cuts, smallest, top_value):
    level = 1.0
    for dim, blocks in cuts:
        heights = jax.random.uniform(jax.random.fold_in(jax.random.fold_in(rng, 6), dim), (blocks,), jnp.float32, smallest / len(cuts), top_value / len(cuts))
        level = level * jnp.repeat(jnp.exp(heights), shape[dim] // blocks).reshape((-1,) + (1,) * (len(shape) - 1 - dim))
    return level


def assign_block(own_key, own, number, rows, count, top, most, slope):
    order = jax.random.permutation(own_key, count)
    heavy_load, ordinary = load_shares(count, rows * top, most, slope, True), load_shares(count, rows * top, most, slope, False)
    places = jnp.arange(count)

    def named(tallies, rotation):
        used = int((tallies > 0).sum())
        fixed = max(1, used // 4)
        passed = fixed + (places - fixed + rotation * (used - fixed)) % max(1, count - fixed)
        return jnp.zeros((count,), jnp.int32).at[order[jnp.where(places < fixed, places, passed)]].set(jnp.asarray(tallies, jnp.int32))

    tallies = jnp.where(number % 4 == 0, named(heavy_load, number // 4), named(ordinary, number - number // 4 - 1))
    mixed = jax.random.permutation(jax.random.fold_in(own, 3), count)
    source_of, sink = mixed[0:count // 2 * 2:2], mixed[1:count // 2 * 2:2]
    slack = jnp.minimum(tallies[source_of] - 1, most - tallies[sink]) // 2
    slack = jnp.where((source_of == order[0]) | (sink == order[0]) | (tallies[sink] == 0), 0, jnp.maximum(slack, 0))
    passed = jax.random.randint(jax.random.fold_in(own, 4), (count // 2,), 0, 1 << 20) % (slack + 1)
    tallies = tallies.at[source_of].add(-passed).at[sink].add(passed)
    members = jnp.searchsorted(jnp.cumsum(tallies), jnp.arange(rows * top), side="right").astype(jnp.int32)
    listing = members.reshape(top, rows).T
    listing = listing[jax.random.permutation(jax.random.fold_in(own, 1), rows)]
    rotation = jax.random.randint(jax.random.fold_in(own, 2), (rows, 1), 0, top)
    return jnp.take_along_axis(listing, (jnp.arange(top)[None, :] + rotation) % top, axis=1)


def load_shares(amount, total, most, slope, full):
    weights = [(1 << 20) // math.isqrt(standing ** slope) + 1 for standing in range(1, amount + 1)]
    largest = most if full else min(most, max(-(-total // amount), total * weights[0] // sum(weights)))
    least = 1 if total - largest >= amount - 1 else 0
    holding, rest = [largest] + [least] * (amount - 1), total - largest - least * (amount - 1)
    while rest > 0:
        free = [i for i in range(1, amount) if holding[i] < largest] or [i for i in range(1, amount) if holding[i] < most]
        pool, remaining = sum([weights[i] for i in free]), rest
        for i in free:
            extra = min(most - holding[i], max(1, remaining * weights[i] // pool), rest)
            holding[i] = holding[i] + extra
            rest = rest - extra
    return np.array(holding)


def centred(stream_key, shape, width, reach, split=(), kind=jnp.bfloat16):
    drawn = jax.random.normal(stream_key, shape, jnp.float32) * width
    if len(split) > 0:
        drawn = levels(stream_key, shape, split, -0.22, 0.18) * drawn
    return jnp.clip(drawn, min=-reach, max=reach).astype(kind)


def setup_inputs(seed: int = 0) -> dict:
    key_of = jax.random.split(jax.random.key(seed), 5)
    src_fields = centred(key_of[0], (ELEMS, FIELDS * NB), 1.0, 6.0, ((0, 256),), jnp.float32)
    owner_peer_keys = jax.random.split(jax.random.fold_in(key_of[1], 1), ELEMS * OVL // (8 * E_DEV))
    owner_peer_turns = jax.random.permutation(jax.random.fold_in(key_of[1], 3), ELEMS * OVL // (8 * E_DEV))
    owner_peer = jax.vmap(lambda own, number: assign_block(jax.random.fold_in(key_of[1], 2), own, number, 8 * E_DEV, GROUP, 1, CAP, 2))(owner_peer_keys, owner_peer_turns).reshape((ELEMS, OVL, 1))
    src_local = touch_ends(jax.random.randint(key_of[2], (ELEMS, OVL), 0, E_DEV), jax.random.fold_in(key_of[2], 1), 0, E_DEV - 1).astype(jnp.int32)
    jac = jnp.clip(jnp.exp(math.log(4.0) - 2.7725887 * jax.random.uniform(key_of[3], (ELEMS, OVL * QP), jnp.float32) ** levels(key_of[3], (ELEMS, OVL * QP), ((0, 256),), -0.2, 0.2)), 0.25, 4.0)
    return {"src_fields": src_fields, "owner_peer": owner_peer, "src_local": src_local, "jac": jac}


def bern_table(points):
    cols = [math.comb(5, i) * points ** i * (1.0 - points) ** (5 - i) for i in range(6)]
    return np.stack(cols, -1)


def remap_tables():
    mids = (np.arange(8) + 0.5) / 16.0
    src_one = []
    tgt_one = []
    for bit in range(2):
        target_pts = bit * 0.5 + mids
        source_pts = target_pts + 0.5 - bit
        src_one.append(bern_table(source_pts).T)
        tgt_one.append(bern_table(target_pts) / 16.0)
    source_list = []
    project_list = []
    for intersection in range(8):
        bit_x, bit_y, bit_z = (intersection >> 2) & 1, (intersection >> 1) & 1, intersection & 1
        source_list.append(np.kron(src_one[bit_x], np.kron(src_one[bit_y], src_one[bit_z])))
        project_list.append(np.kron(tgt_one[bit_x], np.kron(tgt_one[bit_y], tgt_one[bit_z])))
    return jnp.asarray(np.stack(source_list), jnp.float32), jnp.asarray(np.stack(project_list), jnp.float32)


def lower_integral(first, second):
    if first < 0 or first > 4:
        return 0.0
    return math.comb(4, first) * math.comb(5, second) / (10.0 * math.comb(9, first + second))


def force_table():
    mass_one = np.zeros((6, 6))
    grad_one = np.zeros((6, 6))
    for left in range(6):
        for right in range(6):
            mass_one[left, right] = math.comb(5, left) * math.comb(5, right) / (11.0 * math.comb(10, left + right))
            grad_one[left, right] = 5.0 * (lower_integral(left - 1, right) - lower_integral(left, right))
    grad_x = np.kron(grad_one, np.kron(mass_one, mass_one))
    grad_y = np.kron(mass_one, np.kron(grad_one, mass_one))
    grad_z = np.kron(mass_one, np.kron(mass_one, grad_one))
    joined = np.concatenate([grad_x.T, grad_y.T, grad_z.T], 1) * 8.0
    return jnp.asarray(joined, jnp.float32)


def remap_block(fetch_rows, weights, source_tab, project_tab, force_tab):
    count = weights.shape[0]
    hi = lax.Precision.HIGHEST
    total = jnp.zeros((count * FIELDS, NB), jnp.float32)
    for intersection in range(OVL):
        rows = fetch_rows(intersection).reshape(count * FIELDS, NB)
        values = jnp.dot(rows, source_tab[intersection], precision=hi)
        scaled = values.reshape(count, FIELDS, QP) * weights[:, None, intersection * QP:(intersection + 1) * QP]
        total = total + jnp.dot(scaled.reshape(count * FIELDS, QP), project_tab[intersection], precision=hi)
    lumped = jnp.dot(weights, project_tab.reshape(OVL * QP, NB), precision=hi)
    fields = total.reshape(count, FIELDS, NB) / lumped[:, None, :]
    pressure = fields[:, 0, :] * fields[:, 1, :]
    force = jnp.dot(pressure, force_tab, precision=hi)
    parts = jnp.concatenate([force.reshape(count, 3, NB), lumped[:, None, :]], 1)
    return fields.reshape(count, FIELDS * NB), parts


def spread(field, elem_axis, node_axis):
    moved = jnp.moveaxis(field, (elem_axis, node_axis), (-2, -1))
    count = moved.shape[-2]
    lead = moved.shape[:-2]
    lower = moved[..., :5].reshape(lead + (5 * count,))
    upper = jnp.concatenate([jnp.zeros(lead + (count, 4), moved.dtype), moved[..., 5:]], -1).reshape(lead + (5 * count,))
    spec = [(0, 0)] * len(lead)
    lattice = jnp.pad(lower, spec + [(0, 1)]) + jnp.pad(upper, spec + [(1, 0)])
    return jnp.moveaxis(lattice, -1, elem_axis)


def unspread(lattice, axis):
    moved = jnp.moveaxis(lattice, axis, -1)
    count = (moved.shape[-1] - 1) // 5
    lead = moved.shape[:-1]
    lower = moved[..., :5 * count].reshape(lead + (count, 5))
    last = moved[..., 5::5][..., None]
    nodes = jnp.concatenate([lower, last], -1)
    return jnp.moveaxis(nodes, -2, axis)


def reference(src_fields, owner_peer, src_local, jac):
    source_tab, project_tab = remap_tables()
    force_tab = force_table()
    blocks = ELEMS // E_DEV
    row_ids = jnp.arange(ELEMS, dtype=jnp.int32)
    zpos = (row_ids // E_DEV) % N_GZ
    source_row = (owner_peer[:, :, 0] * N_GZ + zpos[:, None]) * E_DEV + src_local

    def one_block(packed):
        index_rows, weights = packed

        def fetch_rows(intersection):
            return jnp.take(src_fields, index_rows[:, intersection], axis=0)

        return remap_block(fetch_rows, weights, source_tab, project_tab, force_tab)

    fields, parts = lax.map(one_block, (source_row.reshape(blocks, E_DEV, OVL), jac.reshape(blocks, E_DEV, OVL * QP)))
    remapped = fields.reshape(ELEMS, FIELDS * NB)
    grid = parts.reshape(N_GX, N_GY, N_GZ, EX, EY, EZ, 4, 6, 6, 6)
    grid = jnp.transpose(grid, (6, 0, 3, 1, 4, 2, 5, 7, 8, 9)).reshape(4, N_GX * EX, N_GY * EY, N_GZ * EZ, 6, 6, 6)
    lattice = spread(spread(spread(grid, 1, 4), 2, 4), 3, 4)
    accel = lattice[:3] / lattice[3:4]
    back = unspread(unspread(unspread(accel, 1), 2), 3)
    back = back.reshape(3, N_GX, EX, N_GY, EY, N_GZ, EZ, NB)
    nodal_accel = jnp.transpose(back, (1, 3, 5, 2, 4, 6, 0, 7)).reshape(ELEMS, 3 * NB)
    return remapped, nodal_accel
```

```python
import math

import jax
import jax.numpy as jnp
import numpy as np
from jax import lax
from jax.sharding import PartitionSpec as P

EX = 4
EY = 4
EZ = 2
FIELDS = 5
NB = 216
QP = 512
OVL = 8


def in_blocks(array, dim, count):
    shape = array.shape
    tiles = array.reshape(*shape[:dim], count, shape[dim] // count, *shape[dim + 1 :])
    return jnp.moveaxis(tiles, dim, 0)


def in_order(tiles, dim):
    shape = list(tiles.shape[1:])
    shape[dim] *= tiles.shape[0]
    return jnp.moveaxis(tiles, 0, dim).reshape(shape)


def joined_exchange(array, axis, axes, splits, concats):
    sizes = [lax.axis_size(a) for a in axes]
    tiles = in_blocks(array, splits[0], sizes[0])
    tiles = jnp.moveaxis(in_blocks(tiles, splits[1] + 1, sizes[1]), 0, 1)
    inside = tiles.shape[2:]
    tiles = tiles.reshape(-1, *inside)
    tiles = lax.all_to_all(tiles, axis, split_axis=0, concat_axis=0, tiled=True)
    tiles = in_order(tiles.reshape(*sizes, *inside), concats[0] + 1)
    return in_order(tiles, concats[1])


def bern_table(points):
    cols = [math.comb(5, i) * points**i * (1.0 - points) ** (5 - i) for i in range(6)]
    return np.stack(cols, -1)


def remap_tables():
    mids = (np.arange(8) + 0.5) / 16.0
    src_one = []
    tgt_one = []
    for bit in range(2):
        target_pts = bit * 0.5 + mids
        source_pts = target_pts + 0.5 - bit
        src_one.append(bern_table(source_pts).T)
        tgt_one.append(bern_table(target_pts) / 16.0)
    source_list = []
    project_list = []
    for intersection in range(8):
        bit_x, bit_y, bit_z = (intersection >> 2 & 1, intersection >> 1 & 1, intersection & 1)
        source_list.append(np.kron(src_one[bit_x], np.kron(src_one[bit_y], src_one[bit_z])))
        project_list.append(np.kron(tgt_one[bit_x], np.kron(tgt_one[bit_y], tgt_one[bit_z])))
    return (
        jnp.asarray(np.stack(source_list), jnp.float32),
        jnp.asarray(np.stack(project_list), jnp.float32),
    )


def lower_integral(first, second):
    if first < 0 or first > 4:
        return 0.0
    return math.comb(4, first) * math.comb(5, second) / (10.0 * math.comb(9, first + second))


def force_table():
    mass_one = np.zeros((6, 6))
    grad_one = np.zeros((6, 6))
    for left in range(6):
        for right in range(6):
            mass_one[left, right] = (
                math.comb(5, left) * math.comb(5, right) / (11.0 * math.comb(10, left + right))
            )
            grad_one[left, right] = 5.0 * (
                lower_integral(left - 1, right) - lower_integral(left, right)
            )
    grad_x = np.kron(grad_one, np.kron(mass_one, mass_one))
    grad_y = np.kron(mass_one, np.kron(grad_one, mass_one))
    grad_z = np.kron(mass_one, np.kron(mass_one, grad_one))
    joined = np.concatenate([grad_x.T, grad_y.T, grad_z.T], 1) * 8.0
    return jnp.asarray(joined, jnp.float32)


def meet(grid, axis, elem_dim, coef_dim):
    count = lax.axis_size(axis)
    length = grid.shape[elem_dim]
    low = lax.slice_in_dim(grid, 0, 1, axis=coef_dim)
    high = lax.slice_in_dim(grid, 5, 6, axis=coef_dim)
    inner = lax.slice_in_dim(grid, 1, 5, axis=coef_dim)
    up = [(i, i + 1) for i in range(count - 1)]
    down = [(i + 1, i) for i in range(count - 1)]
    from_below = lax.ppermute(lax.slice_in_dim(high, length - 1, length, axis=elem_dim), axis, up)
    from_above = lax.ppermute(lax.slice_in_dim(low, 0, 1, axis=elem_dim), axis, down)
    lower = jnp.concatenate(
        [from_below, lax.slice_in_dim(high, 0, length - 1, axis=elem_dim)], elem_dim
    )
    upper = jnp.concatenate([lax.slice_in_dim(low, 1, length, axis=elem_dim), from_above], elem_dim)
    return jnp.concatenate([low + lower, inner, high + upper], coef_dim)


def per_device(src_fields, owner_peer, src_local, jac):
    hi = lax.Precision.HIGHEST
    source_tab, project_tab = remap_tables()
    force_tab = force_table()
    group = lax.axis_size("gx") * lax.axis_size("gy")
    elems = src_fields.shape[0]
    width = src_fields.shape[1]
    capacity = max(2, 9 * elems // group)
    peer_ids = owner_peer.reshape(-1)
    wanted = src_local.reshape(-1)
    peer_hits = (peer_ids[:, None] == jnp.arange(group, dtype=jnp.int32)[None, :]).astype(jnp.int32)
    count = peer_ids.shape[0]
    before = jnp.arange(count)[:, None] > jnp.arange(count)[None, :]
    earlier = jnp.dot(
        before.astype(jnp.bfloat16),
        peer_hits.astype(jnp.bfloat16),
        preferred_element_type=jnp.float32,
    ).astype(jnp.int32)
    rank_in = jnp.sum(earlier * peer_hits, 1)
    position = peer_ids * capacity + rank_in
    requests = jnp.zeros((group * capacity,), jnp.int32).at[position].set(wanted)
    asked = joined_exchange(
        requests.reshape(lax.axis_size("gx"), lax.axis_size("gy"), capacity),
        ("gx", "gy"),
        ("gx", "gy"),
        (0, 1),
        (0, 1),
    )
    picked = jnp.take(src_fields, asked, axis=0)
    arrived = joined_exchange(picked, ("gx", "gy"), ("gx", "gy"), (0, 1), (0, 1))
    arrived = arrived.reshape(group * capacity, width)
    fetched = jnp.take(arrived, position, axis=0).reshape(elems, OVL, FIELDS, NB)
    total = jnp.zeros((elems, FIELDS, NB), jnp.float32)
    for intersection in range(OVL):
        values = jnp.einsum(
            "efi,iq->efq", fetched[:, intersection], source_tab[intersection], precision=hi
        )
        scaled = values * jac[:, None, intersection * QP : (intersection + 1) * QP]
        total = total + jnp.einsum("efq,qj->efj", scaled, project_tab[intersection], precision=hi)
    lumped = jnp.dot(jac, project_tab.reshape(OVL * QP, NB), precision=hi)
    fields = total / lumped[:, None, :]
    pressure = fields[:, 0, :] * fields[:, 1, :]
    force = jnp.dot(pressure, force_tab, precision=hi)
    parts = jnp.concatenate([force.reshape(elems, 3, NB), lumped[:, None, :]], 1)
    grid = parts.reshape(EX, EY, EZ, 4, 6, 6, 6)
    grid = jnp.transpose(grid, (3, 0, 1, 2, 4, 5, 6))
    for axis, dim in (("gx", 1), ("gy", 2), ("gz", 3)):
        grid = meet(grid, axis, dim, dim + 3)
    accel = grid[:3] / grid[3:4]
    nodal_accel = jnp.transpose(accel, (1, 2, 3, 0, 4, 5, 6)).reshape(elems, 3 * NB)
    return (fields.reshape(elems, FIELDS * NB), nodal_accel)


def solution(mesh):
    placed = (
        P(("gx", "gy", "gz"), None),
        P(("gx", "gy", "gz"), None, None),
        P(("gx", "gy", "gz"), None),
        P(("gx", "gy", "gz"), None),
    )
    return jax.shard_map(
        per_device,
        mesh=mesh,
        in_specs=placed,
        out_specs=(P(("gx", "gy", "gz"), None), P(("gx", "gy", "gz"), None)),
        check_vma=False,
    )
```

```python
import math

import jax
import jax.numpy as jnp
import ml_dtypes
import numpy as np
from jax import lax
from jax.experimental import pallas as pl
from jax.experimental.pallas import tpu as pltpu
from jax.sharding import PartitionSpec as P

EX = 4
EY = 4
EZ = 2
FIELDS = 5
NB = 216
QP = 512
OVL = 8
ELEMS = 32
WIDTH = FIELDS * NB
NX = 4
NY = 8
CAP = 9
SLOTS = NX * NY * CAP
MESH = pl.DeviceIdType.MESH
F32 = jnp.float32
BF16 = jnp.bfloat16


def bern_table(points):
    cols = [math.comb(5, i) * points**i * (1.0 - points) ** (5 - i) for i in range(6)]
    return np.stack(cols, -1)


def remap_tables():
    mids = (np.arange(8) + 0.5) / 16.0
    src_one = []
    tgt_one = []
    for bit in range(2):
        target_pts = bit * 0.5 + mids
        source_pts = target_pts + 0.5 - bit
        src_one.append(bern_table(source_pts).T)
        tgt_one.append(bern_table(target_pts) / 16.0)
    source_list = []
    project_list = []
    for intersection in range(8):
        bit_x, bit_y, bit_z = (intersection >> 2 & 1, intersection >> 1 & 1, intersection & 1)
        source_list.append(np.kron(src_one[bit_x], np.kron(src_one[bit_y], src_one[bit_z])))
        project_list.append(np.kron(tgt_one[bit_x], np.kron(tgt_one[bit_y], tgt_one[bit_z])))
    return np.stack(source_list), np.stack(project_list)


def lower_integral(first, second):
    if first < 0 or first > 4:
        return 0.0
    return math.comb(4, first) * math.comb(5, second) / (10.0 * math.comb(9, first + second))


def force_table():
    mass_one = np.zeros((6, 6))
    grad_one = np.zeros((6, 6))
    for left in range(6):
        for right in range(6):
            mass_one[left, right] = (
                math.comb(5, left) * math.comb(5, right) / (11.0 * math.comb(10, left + right))
            )
            grad_one[left, right] = 5.0 * (
                lower_integral(left - 1, right) - lower_integral(left, right)
            )
    grad_x = np.kron(grad_one, np.kron(mass_one, mass_one))
    grad_y = np.kron(mass_one, np.kron(grad_one, mass_one))
    grad_z = np.kron(mass_one, np.kron(mass_one, grad_one))
    padded = [np.pad(g.T * 8.0, ((0, 0), (0, 40))) for g in (grad_x, grad_y, grad_z)]
    return np.concatenate(padded, 1)


def two_parts(table):
    high = table.astype(ml_dtypes.bfloat16)
    low = (table - high.astype(np.float64)).astype(ml_dtypes.bfloat16)
    return high, low


def halves(x):
    high = x.astype(BF16)
    return high, (x - high.astype(F32)).astype(BF16)


def dot3(a_high, a_low, b_high, b_low):
    total = jnp.dot(a_high, b_high, preferred_element_type=F32)
    total += jnp.dot(a_low, b_high, preferred_element_type=F32)
    return total + jnp.dot(a_high, b_low, preferred_element_type=F32)


def fetch_kernel(
    src_ref, owner_ref, local_ref, out_ref,
    b1, b2, b3, b4, b5, b6, b7, send, arr, req_v, rreq_v, pos_v, req_s, pos_s,
    ring_send, ring_recv, req_send, req_recv, row_send, row_recv, copy_sem,
):
    x = lax.axis_index("gx")
    z = lax.axis_index("gy")
    right = lax.rem(z + 1, NY)
    left = lax.rem(z + NY - 1, NY)
    ahead = [lax.rem(x + i, NX) for i in range(NX)]
    blk = [src_ref, b1, b2, b3, b4, b5, b6, b7]

    barrier = pltpu.get_barrier_semaphore()
    for axis, where in (("gy", left), ("gy", right), ("gx", ahead[1]), ("gx", ahead[2]), ("gx", ahead[3])):
        pl.semaphore_signal(barrier, inc=1, device_id={axis: where}, device_id_type=MESH)
    pl.semaphore_wait(barrier, 5)

    def hop(way, d, c):
        dst = (d + 1) % 8 if way == 0 else (d + 7) % 8
        rows = pl.ds(16 * c, 16)
        return pltpu.make_async_remote_copy(
            src_ref=blk[d].at[rows],
            dst_ref=blk[dst].at[rows],
            send_sem=ring_send.at[way, d, c],
            recv_sem=ring_recv.at[way, dst, c],
            device_id={"gy": right if way == 0 else left},
            device_id_type=MESH,
        )

    hops = []

    def go(way, d, c):
        one = hop(way, d, c)
        one.start()
        hops.append(one)

    def arrived(way, d, c):
        hop(way, (d + 7) % 8 if way == 0 else (d + 1) % 8, c).wait_recv()

    for c in range(2):
        go(0, 0, c)
        go(1, 0, c)

    count = ELEMS * OVL
    owner = owner_ref[...].reshape(count, 1)
    xrel = (owner // 8 - x + NX) & 3
    back = (z - (owner & 7) + NY) & 7
    group = xrel * 8 + back
    rows_i = lax.broadcasted_iota(jnp.int32, (count, 32), 0)
    cols_i = lax.broadcasted_iota(jnp.int32, (count, 32), 1)
    hits = jnp.where(group == cols_i, 1.0, 0.0)
    tri = lax.broadcasted_iota(jnp.int32, (count, count), 0) > lax.broadcasted_iota(
        jnp.int32, (count, count), 1
    )
    earlier = jnp.dot(
        jnp.where(tri, 1.0, 0.0).astype(BF16), hits.astype(BF16), preferred_element_type=F32
    )
    rank = jnp.sum(earlier * hits, 1, keepdims=True)
    own_row = jnp.where(rows_i // 8 == cols_i, 1.0, 0.0).astype(BF16)
    spread_local = jnp.dot(
        own_row, local_ref[...].astype(F32).astype(BF16), preferred_element_type=F32
    )
    mine = (rows_i[:, :8] & 7) == cols_i[:, :8]
    wanted = jnp.sum(jnp.where(mine, spread_local, 0.0), 1, keepdims=True)
    wide = lax.broadcasted_iota(jnp.int32, (count, 128), 1)
    placed = jnp.where(wide == rank.astype(jnp.int32), wanted, 0.0)
    req_v[...] = lax.dot_general(
        hits.astype(BF16), placed.astype(BF16), (((0,), (0,)), ((), ())), preferred_element_type=F32
    ).astype(jnp.int32)

    asks = []
    for i in range(1, NX):
        ask = pltpu.make_async_remote_copy(
            src_ref=req_v.at[pl.ds(8 * i, 8)],
            dst_ref=rreq_v.at[i - 1],
            send_sem=req_send.at[i - 1],
            recv_sem=req_recv.at[i - 1],
            device_id={"gx": ahead[i]},
            device_id_type=MESH,
        )
        ask.start()
        asks.append(ask)
    mine_first = pltpu.make_async_copy(req_v.at[pl.ds(0, 8)], req_s.at[0], copy_sem.at[0])
    mine_first.start()

    position = group.astype(F32) * float(CAP) + jnp.minimum(rank, float(CAP - 1))
    by_row = jnp.where(
        lax.broadcasted_iota(jnp.int32, (count, 128), 0) // 8 == wide, position, 0.0
    )
    pick = lax.broadcasted_iota(jnp.int32, (8, count), 0) == (
        lax.broadcasted_iota(jnp.int32, (8, count), 1) & 7
    )
    pos_v[...] = jnp.dot(
        jnp.where(pick, 1.0, 0.0), by_row, precision=lax.Precision.HIGHEST,
        preferred_element_type=F32,
    ).astype(jnp.int32)
    pos_copy = pltpu.make_async_copy(pos_v, pos_s, copy_sem.at[1])
    pos_copy.start()

    mine_first.wait()
    for i in range(1, NX):
        asks[i - 1].wait_recv()
        one = pltpu.make_async_copy(rreq_v.at[i - 1], req_s.at[i], copy_sem.at[1 + i])
        one.start()
        one.wait()
    pos_copy.wait()

    def reply(i, d):
        return pltpu.make_async_remote_copy(
            src_ref=send.at[pl.ds(((i - 1) * 8 + d) * CAP, CAP)],
            dst_ref=arr.at[pl.ds((i * 8 + d) * CAP, CAP)],
            send_sem=row_send.at[i - 1, d],
            recv_sem=row_recv.at[i - 1, d],
            device_id={"gx": ahead[NX - i]},
            device_id_type=MESH,
        )

    def answer(d):
        def one_slot(s, carry):
            for i in range(NX):
                row = blk[d][pl.ds(req_s[i, d, s] & (ELEMS - 1), 1), :]
                if i == 0:
                    arr[d * CAP + s] = row
                else:
                    send[((i - 1) * 8 + d) * CAP + s] = row
            return carry

        lax.fori_loop(0, CAP, one_slot, 0)
        for i in (1, 3, 2):
            reply(i, d).start()

    answer(0)
    for j in range(1, 4):
        for c in range(2):
            arrived(0, j, c)
            if j < 3 or c == 0:
                go(0, j, c)
            arrived(1, 8 - j, c)
            if j < 3 or c == 1:
                go(1, 8 - j, c)
        answer(j)
        answer(8 - j)
    arrived(0, 4, 0)
    arrived(1, 4, 1)
    answer(4)

    for i in range(1, NX):
        for d in range(8):
            reply(i, d).wait_recv()

    def one_row(r, carry):
        for k in range(OVL):
            out_ref[k, pl.ds(r, 1), :] = arr[jnp.clip(pos_s[k, r], 0, SLOTS - 1)]
        return carry

    lax.fori_loop(0, ELEMS, one_row, 0)

    for one in hops:
        one.wait_send()
    for one in asks:
        one.wait_send()
    for i in range(1, NX):
        for d in range(8):
            reply(i, d).wait_send()


def fetch(src_fields, owner_peer, src_local):
    vmem = pl.BlockSpec(memory_space=pltpu.VMEM)
    dma = pltpu.SemaphoreType.DMA
    return pl.pallas_call(
        fetch_kernel,
        out_shape=jax.ShapeDtypeStruct((OVL, ELEMS, WIDTH), F32),
        in_specs=[vmem] * 3,
        out_specs=vmem,
        scratch_shapes=[pltpu.VMEM((ELEMS, WIDTH), F32) for _ in range(7)]
        + [
            pltpu.VMEM(((NX - 1) * NY * CAP, 1, WIDTH), F32),
            pltpu.VMEM((SLOTS, 1, WIDTH), F32),
            pltpu.VMEM((NX * NY, 128), jnp.int32),
            pltpu.VMEM((NX - 1, NY, 128), jnp.int32),
            pltpu.VMEM((OVL, 128), jnp.int32),
            pltpu.SMEM((NX, NY, 128), jnp.int32),
            pltpu.SMEM((OVL, 128), jnp.int32),
            dma((2, 8, 2)),
            dma((2, 8, 2)),
            dma((NX - 1,)),
            dma((NX - 1,)),
            dma((NX - 1, NY)),
            dma((NX - 1, NY)),
            dma((5,)),
        ],
        compiler_params=pltpu.CompilerParams(
            collective_id=0, has_side_effects=True, vmem_limit_bytes=40 << 20
        ),
        name="fetch_rows",
    )(src_fields, owner_peer, src_local)


def remap_kernel(
    rows_ref, jac_ref, sh_ref, sl_ref, ph_ref, pl_ref, fh_ref, fl_ref, out_ref, parts_ref, acc
):
    k = pl.program_id(0)
    rows = rows_ref[0]
    x = jnp.concatenate([rows[:, f * NB : (f + 1) * NB] for f in range(FIELDS)], 0)
    xh, xl = halves(x)
    values = dot3(xh, xl, sh_ref[0], sl_ref[0])
    weight = jac_ref[...]
    scaled = [values[f * ELEMS : (f + 1) * ELEMS] * weight for f in range(FIELDS)]
    wh, wl = halves(jnp.concatenate(scaled + [weight], 0))
    part = dot3(wh, wl, ph_ref[0], pl_ref[0])

    @pl.when(k == 0)
    def _():
        acc[...] = part

    @pl.when(k > 0)
    def _():
        acc[...] += part

    @pl.when(k == OVL - 1)
    def _():
        lumped = acc[FIELDS * ELEMS :]
        fields = [acc[f * ELEMS : (f + 1) * ELEMS] / lumped for f in range(FIELDS)]
        out_ref[...] = jnp.concatenate(fields, 1)
        qh, ql = halves(fields[0] * fields[1])
        force = dot3(qh, ql, fh_ref[...], fl_ref[...])
        for c in range(3):
            parts_ref[c] = force[:, 256 * c : 256 * (c + 1)]
        parts_ref[3] = jnp.concatenate([lumped, jnp.zeros((ELEMS, 40), F32)], 1)


def remap(rows, jac):
    source_tab, project_tab = remap_tables()
    tables = [*two_parts(source_tab), *two_parts(project_tab), *two_parts(force_table())]
    per_k = lambda shape: pl.BlockSpec((1, *shape), lambda k: (k, 0, 0))
    fixed = pl.BlockSpec((NB, 768), lambda k: (0, 0))
    return pl.pallas_call(
        remap_kernel,
        grid=(OVL,),
        out_shape=(
            jax.ShapeDtypeStruct((ELEMS, WIDTH), F32),
            jax.ShapeDtypeStruct((4, ELEMS, 256), F32),
        ),
        in_specs=[
            per_k((ELEMS, WIDTH)),
            pl.BlockSpec((ELEMS, QP), lambda k: (0, k)),
            per_k((NB, QP)),
            per_k((NB, QP)),
            per_k((QP, NB)),
            per_k((QP, NB)),
            fixed,
            fixed,
        ],
        out_specs=(
            pl.BlockSpec((ELEMS, WIDTH), lambda k: (0, 0)),
            pl.BlockSpec((4, ELEMS, 256), lambda k: (0, 0, 0)),
        ),
        scratch_shapes=[pltpu.VMEM(((FIELDS + 1) * ELEMS, NB), F32)],
        compiler_params=pltpu.CompilerParams(vmem_limit_bytes=60 << 20),
        name="remap",
    )(rows, jac, *[jnp.asarray(t) for t in tables])


def node_kernel(parts_ref, out_ref, *scratch):
    sends, recvs, (send_sem, recv_sem) = scratch[:6], scratch[6:12], scratch[12:]
    place = [lax.axis_index(a) for a in ("gx", "gy", "gz")]
    counts = (NX, NY, 8)
    names = ("gx", "gy", "gz")

    barrier = pltpu.get_barrier_semaphore()
    near = 0
    for dim in range(3):
        for way in (-1, 1):
            there = place[dim] + way
            inside = (there >= 0) & (there < counts[dim])

            @pl.when(inside)
            def _():
                pl.semaphore_signal(
                    barrier, inc=1, device_id={names[dim]: there}, device_id_type=MESH
                )

            near = near + jnp.where(inside, 1, 0)
    pl.semaphore_wait(barrier, near)

    lane = lax.broadcasted_iota(jnp.int32, (4, 4, 8, 256), 3)
    sub = lax.broadcasted_iota(jnp.int32, (4, 4, 8, 256), 2)
    lane_in = (lane // 36, (lane // 6) % 6, lane % 6)
    shifts = (180, 30, 5)
    a = parts_ref[...].reshape(4, 4, 8, 256)

    def roll_sub(v, by):
        return v if by % 8 == 0 else pltpu.roll(v, by % 8, len(v.shape) - 2)

    def pack(dim, a, high):
        if dim == 0:
            return a[:, 3 if high else 0][:, None]
        s = sub[:, :1]
        if dim == 1:
            first = 6 if high else 0
            out = roll_sub(a[:, :1], -first)
            for e in range(1, 4):
                out = jnp.where(s // 2 == e, roll_sub(a[:, e : e + 1], 2 * e - first), out)
            return out
        first = 1 if high else 0
        pairs = [
            jnp.where(
                s % 2 == 0,
                roll_sub(a[:, 2 * e : 2 * e + 1], -first),
                roll_sub(a[:, 2 * e + 1 : 2 * e + 2], 1 - first),
            )
            for e in range(2)
        ]
        return jnp.concatenate(pairs, 1)

    def shifted(dim, a, got, up):
        if dim == 0:
            parts = [a[:, 1:], got] if up else [got, a[:, :3]]
            return jnp.concatenate(parts, 1)
        if dim == 1:
            local = roll_sub(a, -2 if up else 2)
            first = 6 if up else 0
            away = [roll_sub(got, first - 2 * e) for e in range(4)]
            far = sub // 2 == (3 if up else 0)
        else:
            local = roll_sub(a, -1 if up else 1)
            first = 1 if up else 0
            away = [
                roll_sub(got[:, e // 2 : e // 2 + 1], first - e % 2) for e in range(4)
            ]
            far = sub % 2 == (1 if up else 0)
        return jnp.where(far, jnp.concatenate(away, 1), local)

    for dim in range(3):
        copies = []
        for side, way in ((0, -1), (1, 1)):
            n = 2 * dim + side
            there = place[dim] + way
            inside = (there >= 0) & (there < counts[dim])
            copy = pltpu.make_async_remote_copy(
                src_ref=sends[n],
                dst_ref=recvs[2 * dim + 1 - side],
                send_sem=send_sem.at[n],
                recv_sem=recv_sem.at[2 * dim + 1 - side],
                device_id={names[dim]: jnp.clip(there, 0, counts[dim] - 1)},
                device_id_type=MESH,
            )
            sends[n][...] = pack(dim, a, side == 1)

            @pl.when(inside)
            def _():
                copy.start()

            @pl.when(jnp.logical_not(inside))
            def _():
                recvs[n][...] = jnp.zeros_like(recvs[n])

            copies.append((n, inside, copy))
        for side in range(2):
            n, inside, _ = copies[side]
            other = copies[1 - side][2]

            @pl.when(inside)
            def _():
                other.wait_recv()

        up = shifted(dim, a, recvs[2 * dim + 1][...], True)
        down = shifted(dim, a, recvs[2 * dim][...], False)
        by = shifts[dim]
        gain = jnp.where(lane_in[dim] == 5, pltpu.roll(up, by, 3), 0.0)
        gain += jnp.where(lane_in[dim] == 0, pltpu.roll(down, 256 - by, 3), 0.0)
        a = a + gain
        for n, inside, copy in copies:

            @pl.when(inside)
            def _():
                copy.wait_send()

    mass = a[3].reshape(ELEMS, 256)[:, :NB]
    accel = [a[c].reshape(ELEMS, 256)[:, :NB] / mass for c in range(3)]
    out_ref[...] = jnp.concatenate(accel, 1)


def nodes(parts):
    vmem = pl.BlockSpec(memory_space=pltpu.VMEM)
    dma = pltpu.SemaphoreType.DMA
    tiles = [1, 1, 1, 1, 2, 2]
    return pl.pallas_call(
        node_kernel,
        out_shape=jax.ShapeDtypeStruct((ELEMS, 3 * NB), F32),
        in_specs=[vmem],
        out_specs=vmem,
        scratch_shapes=[pltpu.VMEM((4, t, 8, 256), F32) for t in tiles + tiles] + [dma((6,)), dma((6,))],
        compiler_params=pltpu.CompilerParams(
            collective_id=1, has_side_effects=True, vmem_limit_bytes=40 << 20
        ),
        name="node_sums",
    )(parts)


def per_device(src_fields, owner_peer, src_local, jac):
    rows = fetch(src_fields, owner_peer, src_local)
    remapped, parts = remap(rows, jac)
    return remapped, nodes(parts)


def solution(mesh):
    placed = (
        P(("gx", "gy", "gz"), None),
        P(("gx", "gy", "gz"), None, None),
        P(("gx", "gy", "gz"), None),
        P(("gx", "gy", "gz"), None),
    )
    return jax.shard_map(
        per_device,
        mesh=mesh,
        in_specs=placed,
        out_specs=(P(("gx", "gy", "gz"), None), P(("gx", "gy", "gz"), None)),
        check_vma=False,
    )
```

```python
import math

import jax
import jax.numpy as jnp
import ml_dtypes
import numpy as np
from jax import lax
from jax.experimental import pallas as pl
from jax.experimental.pallas import tpu as pltpu
from jax.sharding import PartitionSpec as P

EX = 4
EY = 4
EZ = 2
FIELDS = 5
NB = 216
QP = 512
OVL = 8
ELEMS = 32
WIDTH = FIELDS * NB
NX = 4
NY = 8
NZ = 8
CAP = 9
SLOTS = NX * NY * CAP
MESH = pl.DeviceIdType.MESH
F32 = jnp.float32
BF16 = jnp.bfloat16


def bern_table(points):
    cols = [math.comb(5, i) * points**i * (1.0 - points) ** (5 - i) for i in range(6)]
    return np.stack(cols, -1)


def remap_tables():
    mids = (np.arange(8) + 0.5) / 16.0
    src_one = []
    tgt_one = []
    for bit in range(2):
        target_pts = bit * 0.5 + mids
        source_pts = target_pts + 0.5 - bit
        src_one.append(bern_table(source_pts).T)
        tgt_one.append(bern_table(target_pts) / 16.0)
    source_list = []
    project_list = []
    for intersection in range(8):
        bit_x, bit_y, bit_z = (intersection >> 2 & 1, intersection >> 1 & 1, intersection & 1)
        source_list.append(np.kron(src_one[bit_x], np.kron(src_one[bit_y], src_one[bit_z])))
        project_list.append(np.kron(tgt_one[bit_x], np.kron(tgt_one[bit_y], tgt_one[bit_z])))
    return np.stack(source_list), np.stack(project_list)


def lower_integral(first, second):
    if first < 0 or first > 4:
        return 0.0
    return math.comb(4, first) * math.comb(5, second) / (10.0 * math.comb(9, first + second))


def force_table():
    mass_one = np.zeros((6, 6))
    grad_one = np.zeros((6, 6))
    for left in range(6):
        for right in range(6):
            mass_one[left, right] = (
                math.comb(5, left) * math.comb(5, right) / (11.0 * math.comb(10, left + right))
            )
            grad_one[left, right] = 5.0 * (
                lower_integral(left - 1, right) - lower_integral(left, right)
            )
    grad_x = np.kron(grad_one, np.kron(mass_one, mass_one))
    grad_y = np.kron(mass_one, np.kron(grad_one, mass_one))
    grad_z = np.kron(mass_one, np.kron(mass_one, grad_one))
    padded = [np.pad(g.T * 8.0, ((0, 0), (0, 40))) for g in (grad_x, grad_y, grad_z)]
    return np.concatenate(padded, 1)


def two_parts(table):
    high = table.astype(ml_dtypes.bfloat16)
    low = (table - high.astype(np.float64)).astype(ml_dtypes.bfloat16)
    return high, low


def halves(x):
    high = x.astype(BF16)
    return high, (x - high.astype(F32)).astype(BF16)


def dot3(a_high, a_low, b_high, b_low):
    total = jnp.dot(a_high, b_high, preferred_element_type=F32)
    total += jnp.dot(a_low, b_high, preferred_element_type=F32)
    return total + jnp.dot(a_high, b_low, preferred_element_type=F32)


def roll_sub(v, by):
    return v if by % 8 == 0 else pltpu.roll(v, by % 8, len(v.shape) - 2)


def pack_face(dim, a, high):
    sub = lax.broadcasted_iota(jnp.int32, (4, 1, 8, 256), 2)
    if dim == 0:
        return a[:, 3 if high else 0][:, None]
    if dim == 1:
        first = 6 if high else 0
        out = roll_sub(a[:, :1], -first)
        for e in range(1, 4):
            out = jnp.where(sub // 2 == e, roll_sub(a[:, e : e + 1], 2 * e - first), out)
        return out
    first = 1 if high else 0
    pairs = [
        jnp.where(
            sub % 2 == 0,
            roll_sub(a[:, 2 * e : 2 * e + 1], -first),
            roll_sub(a[:, 2 * e + 1 : 2 * e + 2], 1 - first),
        )
        for e in range(2)
    ]
    return jnp.concatenate(pairs, 1)


def neighbour_rows(dim, a, got, up):
    sub = lax.broadcasted_iota(jnp.int32, (4, 4, 8, 256), 2)
    if dim == 0:
        return jnp.concatenate([a[:, 1:], got] if up else [got, a[:, :3]], 1)
    if dim == 1:
        local = roll_sub(a, -2 if up else 2)
        first = 6 if up else 0
        away = [roll_sub(got, first - 2 * e) for e in range(4)]
        far = sub // 2 == (3 if up else 0)
    else:
        local = roll_sub(a, -1 if up else 1)
        first = 1 if up else 0
        away = [roll_sub(got[:, e // 2 : e // 2 + 1], first - e % 2) for e in range(4)]
        far = sub % 2 == (1 if up else 0)
    return jnp.where(far, jnp.concatenate(away, 1), local)


def whole_kernel(
    src_hbm, owner_ref, local_ref, jac_hbm, sh_hbm, sl_hbm, ph_hbm, pl_hbm, fh_hbm, fl_hbm,
    remapped_ref, accel_ref,
    b0, b1, b2, b3, b4, b5, b6, b7, send, arr, req_v, rreq_v, pos_v, req_s, pos_s,
    jac_v, sh_v, sl_v, ph_v, pl_v, fh_v, fl_v, rows_v,
    s0, s1, s2, s3, s4, s5, r0, r1, r2, r3, r4, r5,
    ring_send, ring_recv, req_send, req_recv, row_send, row_recv, copy_sem, load_sem,
    face_send, face_recv,
):
    x = lax.axis_index("gx")
    z = lax.axis_index("gy")
    y = lax.axis_index("gz")
    right = lax.rem(z + 1, NY)
    left = lax.rem(z + NY - 1, NY)
    ahead = [lax.rem(x + i, NX) for i in range(NX)]
    blk = [b0, b1, b2, b3, b4, b5, b6, b7]
    sends = [s0, s1, s2, s3, s4, s5]
    recvs = [r0, r1, r2, r3, r4, r5]
    place = (x, z, y)
    counts = (NX, NY, NZ)
    names = ("gx", "gy", "gz")

    def there(dim, side):
        return place[dim] + 2 * side - 1

    def inside(dim, side):
        return place[dim] < counts[dim] - 1 if side else place[dim] > 0

    barrier = pltpu.get_barrier_semaphore()
    for axis, where in (("gy", left), ("gy", right), ("gx", ahead[1]), ("gx", ahead[2]), ("gx", ahead[3])):
        pl.semaphore_signal(barrier, inc=1, device_id={axis: where}, device_id_type=MESH)
    near = 5
    for side in range(2):

        @pl.when(inside(2, side))
        def _():
            pl.semaphore_signal(
                barrier, inc=1, device_id={"gz": there(2, side)}, device_id_type=MESH
            )

        near = near + jnp.where(inside(2, side), 1, 0)

    own_load = pltpu.make_async_copy(src_hbm, b0, load_sem.at[0])
    own_load.start()
    loads = [
        pltpu.make_async_copy(a, b, load_sem.at[1 + i])
        for i, (a, b) in enumerate(
            zip(
                (jac_hbm, sh_hbm, sl_hbm, ph_hbm, pl_hbm, fh_hbm, fl_hbm),
                (jac_v, sh_v, sl_v, ph_v, pl_v, fh_v, fl_v),
            )
        )
    ]

    count = ELEMS * OVL
    owner = jnp.concatenate([owner_ref[k] for k in range(OVL)], 1)
    wanted = jnp.concatenate([local_ref[k : k + 1, :] for k in range(OVL)], 1).astype(F32)
    group = ((owner // NY - x + NX) & 3) * NY + ((z - (owner & 7) + NY) & 7)
    hits = jnp.where(group == lax.broadcasted_iota(jnp.int32, (NX * NY, count), 0), 1.0, 0.0)
    tri = lax.broadcasted_iota(jnp.int32, (count, count), 0) < lax.broadcasted_iota(
        jnp.int32, (count, count), 1
    )
    earlier = jnp.dot(
        hits.astype(BF16), jnp.where(tri, 1.0, 0.0).astype(BF16), preferred_element_type=F32
    )
    rank = jnp.sum(earlier * hits, 0, keepdims=True).astype(jnp.int32)
    slot = lax.broadcasted_iota(jnp.int32, (128, count), 0)
    placed = jnp.where(slot == rank, wanted, 0.0)
    req_v[...] = lax.dot_general(
        hits.astype(BF16), placed.astype(BF16), (((1,), (1,)), ((), ())), preferred_element_type=F32
    ).astype(jnp.int32)
    pos_v[...] = group * CAP + jnp.minimum(rank, CAP - 1)

    pl.semaphore_wait(barrier, near)

    def ask(i):
        return pltpu.make_async_remote_copy(
            src_ref=req_v.at[pl.ds(8 * i, 8)],
            dst_ref=rreq_v.at[i - 1],
            send_sem=req_send.at[i - 1],
            recv_sem=req_recv.at[i - 1],
            device_id={"gx": ahead[i]},
            device_id_type=MESH,
        )

    for i in range(1, NX):
        ask(i).start()

    def hop(way, d, c):
        dst = (d + 1) % 8 if way == 0 else (d + 7) % 8
        rows = pl.ds(16 * c, 16)
        return pltpu.make_async_remote_copy(
            src_ref=blk[d].at[rows],
            dst_ref=blk[dst].at[rows],
            send_sem=ring_send.at[way, d, c],
            recv_sem=ring_recv.at[way, dst, c],
            device_id={"gy": right if way == 0 else left},
            device_id_type=MESH,
        )

    hops = []

    def go(way, d, c):
        one = hop(way, d, c)
        one.start()
        hops.append(one)

    def arrived(way, d, c):
        hop(way, (d + 7) % 8 if way == 0 else (d + 1) % 8, c).wait_recv()

    own_load.wait()
    for c in range(2):
        go(0, 0, c)
        go(1, 0, c)
    mine_first = pltpu.make_async_copy(req_v.at[pl.ds(0, 8)], req_s.at[0], copy_sem.at[0])
    mine_first.start()
    pos_copy = pltpu.make_async_copy(pos_v, pos_s, copy_sem.at[4])
    pos_copy.start()
    for one in loads:
        one.start()
    for dim in range(3):
        for side in range(2):

            @pl.when(jnp.logical_not(inside(dim, side)))
            def _():
                recvs[2 * dim + side][...] = jnp.zeros_like(recvs[2 * dim + side])

    mine_first.wait()
    pos_copy.wait()
    for i in range(1, NX):
        ask(i).wait_recv()
        one = pltpu.make_async_copy(rreq_v.at[i - 1], req_s.at[i], copy_sem.at[i])
        one.start()
        one.wait()

    def reply(i, d):
        return pltpu.make_async_remote_copy(
            src_ref=send.at[pl.ds(((i - 1) * 8 + d) * CAP, CAP)],
            dst_ref=arr.at[pl.ds((i * 8 + d) * CAP, CAP)],
            send_sem=row_send.at[i - 1, d],
            recv_sem=row_recv.at[i - 1, d],
            device_id={"gx": ahead[NX - i]},
            device_id_type=MESH,
        )

    def answer(d):
        def one_slot(s, carry):
            for i in range(NX):
                row = blk[d][pl.ds(req_s[i, d, s] & (ELEMS - 1), 1), :]
                if i == 0:
                    arr[d * CAP + s] = row
                else:
                    send[((i - 1) * 8 + d) * CAP + s] = row
            return carry

        lax.fori_loop(0, CAP, one_slot, 0)
        for i in (2, 1, 3):
            reply(i, d).start()

    answer(0)
    for j in range(1, 4):
        for c in range(2):
            arrived(0, j, c)
            if j < 3 or c == 0:
                go(0, j, c)
            arrived(1, 8 - j, c)
            if j < 3 or c == 1:
                go(1, 8 - j, c)
        answer(j)
        answer(8 - j)
    arrived(0, 4, 0)
    arrived(1, 4, 1)
    answer(4)

    for one in loads:
        one.wait()
    for i in range(1, NX):
        for d in range(8):
            reply(i, d).wait_recv()

    total = jnp.zeros(((FIELDS + 1) * ELEMS, NB), F32)
    for k in range(OVL):
        buf = rows_v.at[k % 2]
        for r in range(ELEMS):
            buf[pl.ds(r, 1), :] = arr[jnp.clip(pos_s[0, k * ELEMS + r], 0, SLOTS - 1)]
        rows = buf[...]
        lhs = jnp.concatenate([rows[:, f * NB : (f + 1) * NB] for f in range(FIELDS)], 0)
        values = dot3(*halves(lhs), sh_v[k], sl_v[k])
        weight = jac_v[:, k * QP : (k + 1) * QP]
        scaled = [values[f * ELEMS : (f + 1) * ELEMS] * weight for f in range(FIELDS)]
        total += dot3(*halves(jnp.concatenate(scaled + [weight], 0)), ph_v[k], pl_v[k])
    lumped = total[FIELDS * ELEMS :]
    fields = [total[f * ELEMS : (f + 1) * ELEMS] / lumped for f in range(FIELDS)]
    remapped_ref[...] = jnp.concatenate(fields, 1)
    force = dot3(*halves(fields[0] * fields[1]), fh_v[...], fl_v[...])
    mass = jnp.concatenate([lumped, jnp.zeros((ELEMS, 40), F32)], 1)
    a = jnp.stack([force[:, :256], force[:, 256:512], force[:, 512:], mass], 0)
    a = a.reshape(4, 4, 8, 256)

    lane = lax.broadcasted_iota(jnp.int32, (4, 4, 8, 256), 3)
    lane_in = (lane // 36, (lane // 6) % 6, lane % 6)

    def face(dim, side):
        n = 2 * dim + side
        return pltpu.make_async_remote_copy(
            src_ref=sends[n],
            dst_ref=recvs[2 * dim + 1 - side],
            send_sem=face_send.at[n],
            recv_sem=face_recv.at[2 * dim + 1 - side],
            device_id={names[dim]: jnp.clip(there(dim, side), 0, counts[dim] - 1)},
            device_id_type=MESH,
        )

    for dim in range(3):
        for side in range(2):
            sends[2 * dim + side][...] = pack_face(dim, a, side == 1)

            @pl.when(inside(dim, side))
            def _():
                face(dim, side).start()

        for side in range(2):

            @pl.when(inside(dim, side))
            def _():
                face(dim, 1 - side).wait_recv()

        by = (180, 30, 5)[dim]
        up = neighbour_rows(dim, a, recvs[2 * dim + 1][...], True)
        down = neighbour_rows(dim, a, recvs[2 * dim][...], False)
        gain = jnp.where(lane_in[dim] == 5, pltpu.roll(up, by, 3), 0.0)
        gain += jnp.where(lane_in[dim] == 0, pltpu.roll(down, 256 - by, 3), 0.0)
        a = a + gain

    mass = a[3].reshape(ELEMS, 256)[:, :NB]
    accel = [a[c].reshape(ELEMS, 256)[:, :NB] / mass for c in range(3)]
    accel_ref[...] = jnp.concatenate(accel, 1)

    for dim in range(3):
        for side in range(2):

            @pl.when(inside(dim, side))
            def _():
                face(dim, side).wait_send()

    for one in hops:
        one.wait_send()
    for i in range(1, NX):
        ask(i).wait_send()
        for d in range(8):
            reply(i, d).wait_send()


def per_device(src_fields, owner_peer, src_local, jac):
    source_tab, project_tab = remap_tables()
    tables = [*two_parts(source_tab), *two_parts(project_tab), *two_parts(force_table())]
    vmem = pl.BlockSpec(memory_space=pltpu.VMEM)
    hbm = pl.BlockSpec(memory_space=pltpu.HBM)
    dma = pltpu.SemaphoreType.DMA
    tiles = [1, 1, 1, 1, 2, 2]
    return pl.pallas_call(
        whole_kernel,
        out_shape=(
            jax.ShapeDtypeStruct((ELEMS, WIDTH), F32),
            jax.ShapeDtypeStruct((ELEMS, 3 * NB), F32),
        ),
        in_specs=[hbm, vmem, vmem] + [hbm] * 7,
        out_specs=(vmem, vmem),
        scratch_shapes=[pltpu.VMEM((ELEMS, WIDTH), F32) for _ in range(8)]
        + [
            pltpu.VMEM(((NX - 1) * NY * CAP, 1, WIDTH), F32),
            pltpu.VMEM((SLOTS, 1, WIDTH), F32),
            pltpu.VMEM((NX * NY, 128), jnp.int32),
            pltpu.VMEM((NX - 1, NY, 128), jnp.int32),
            pltpu.VMEM((1, OVL * ELEMS), jnp.int32),
            pltpu.SMEM((NX, NY, 128), jnp.int32),
            pltpu.SMEM((1, OVL * ELEMS), jnp.int32),
            pltpu.VMEM((ELEMS, OVL * QP), F32),
            pltpu.VMEM((OVL, NB, QP), BF16),
            pltpu.VMEM((OVL, NB, QP), BF16),
            pltpu.VMEM((OVL, QP, NB), BF16),
            pltpu.VMEM((OVL, QP, NB), BF16),
            pltpu.VMEM((NB, 768), BF16),
            pltpu.VMEM((NB, 768), BF16),
            pltpu.VMEM((2, ELEMS, WIDTH), F32),
        ]
        + [pltpu.VMEM((4, t, 8, 256), F32) for t in tiles + tiles]
        + [
            dma((2, 8, 2)),
            dma((2, 8, 2)),
            dma((NX - 1,)),
            dma((NX - 1,)),
            dma((NX - 1, NY)),
            dma((NX - 1, NY)),
            dma((5,)),
            dma((8,)),
            dma((6,)),
            dma((6,)),
        ],
        compiler_params=pltpu.CompilerParams(
            collective_id=0, has_side_effects=True, vmem_limit_bytes=58 << 20
        ),
        name="whole",
    )(
        src_fields,
        jnp.transpose(owner_peer, (1, 2, 0)),
        jnp.transpose(src_local, (1, 0)),
        jac,
        *[jnp.asarray(t) for t in tables],
    )


def solution(mesh):
    placed = (
        P(("gx", "gy", "gz"), None),
        P(("gx", "gy", "gz"), None, None),
        P(("gx", "gy", "gz"), None),
        P(("gx", "gy", "gz"), None),
    )
    return jax.shard_map(
        per_device,
        mesh=mesh,
        in_specs=placed,
        out_specs=(P(("gx", "gy", "gz"), None), P(("gx", "gy", "gz"), None)),
        check_vma=False,
    )
```

```python
import math

import jax
import jax.numpy as jnp
import ml_dtypes
import numpy as np
from jax import lax
from jax.experimental import pallas as pl
from jax.experimental.pallas import tpu as pltpu
from jax.sharding import PartitionSpec as P

EX = 4
EY = 4
EZ = 2
FIELDS = 5
NB = 216
QP = 512
OVL = 8
ELEMS = 32
WIDTH = FIELDS * NB
WA = 512
WB = 640
TAIL = WA - 2 * NB
NX = 4
NY = 8
NZ = 8
CAP = 9
SLOTS = NX * NY * CAP
MESH = pl.DeviceIdType.MESH
OFFSETS = [
    (i, j, k) for i in (-1, 1, 0) for j in (-1, 1, 0) for k in (-1, 1, 0) if (i, j, k) != (0, 0, 0)
]
F32 = jnp.float32
BF16 = jnp.bfloat16


def bern_table(points):
    cols = [math.comb(5, i) * points**i * (1.0 - points) ** (5 - i) for i in range(6)]
    return np.stack(cols, -1)


def remap_tables():
    mids = (np.arange(8) + 0.5) / 16.0
    src_one = []
    tgt_one = []
    for bit in range(2):
        target_pts = bit * 0.5 + mids
        source_pts = target_pts + 0.5 - bit
        src_one.append(bern_table(source_pts).T)
        tgt_one.append(bern_table(target_pts) / 16.0)
    source_list = []
    project_list = []
    for intersection in range(8):
        bit_x, bit_y, bit_z = (intersection >> 2 & 1, intersection >> 1 & 1, intersection & 1)
        source_list.append(np.kron(src_one[bit_x], np.kron(src_one[bit_y], src_one[bit_z])))
        project_list.append(np.kron(tgt_one[bit_x], np.kron(tgt_one[bit_y], tgt_one[bit_z])))
    return np.stack(source_list), np.stack(project_list)


def lower_integral(first, second):
    if first < 0 or first > 4:
        return 0.0
    return math.comb(4, first) * math.comb(5, second) / (10.0 * math.comb(9, first + second))


def force_table():
    mass_one = np.zeros((6, 6))
    grad_one = np.zeros((6, 6))
    for left in range(6):
        for right in range(6):
            mass_one[left, right] = (
                math.comb(5, left) * math.comb(5, right) / (11.0 * math.comb(10, left + right))
            )
            grad_one[left, right] = 5.0 * (
                lower_integral(left - 1, right) - lower_integral(left, right)
            )
    grad_x = np.kron(grad_one, np.kron(mass_one, mass_one))
    grad_y = np.kron(mass_one, np.kron(grad_one, mass_one))
    grad_z = np.kron(mass_one, np.kron(mass_one, grad_one))
    padded = [np.pad(g.T * 8.0, ((0, 0), (0, 40))) for g in (grad_x, grad_y, grad_z)]
    return np.concatenate(padded, 1)


def two_parts(table):
    high = table.astype(ml_dtypes.bfloat16)
    low = (table - high.astype(np.float64)).astype(ml_dtypes.bfloat16)
    return high, low


def dot3(x, b_high, b_low):
    high = x.astype(BF16)
    low = (x - high.astype(F32)).astype(BF16)
    rows = x.shape[0]
    first = jnp.dot(jnp.concatenate([high, low], 0), b_high, preferred_element_type=F32)
    return first[:rows] + first[rows:] + jnp.dot(high, b_low, preferred_element_type=F32)


def roll_sub(v, by):
    return v if by % 8 == 0 else pltpu.roll(v, by % 8, len(v.shape) - 2)


def roll_lane(v, by):
    return v if by % 256 == 0 else pltpu.roll(v, by % 256, len(v.shape) - 1)


def shared_inside(dim, a):
    lane = lax.broadcasted_iota(jnp.int32, a.shape, 3)
    sub = lax.broadcasted_iota(jnp.int32, a.shape, 2)
    if dim == 0:
        edge = jnp.zeros_like(a[:, :1])
        up, down = jnp.concatenate([a[:, 1:], edge], 1), jnp.concatenate([edge, a[:, :3]], 1)
    elif dim == 1:
        up = jnp.where(sub // 2 == 3, 0.0, roll_sub(a, -2))
        down = jnp.where(sub // 2 == 0, 0.0, roll_sub(a, 2))
    else:
        up = jnp.where(sub % 2 == 1, 0.0, roll_sub(a, -1))
        down = jnp.where(sub % 2 == 0, 0.0, roll_sub(a, 1))
    step = (36, 6, 1)[dim]
    at = (lane // step) % 6
    gain = jnp.where(at == 5, roll_lane(up, 5 * step), 0.0)
    return a + gain + jnp.where(at == 0, roll_lane(down, -5 * step), 0.0)


def pack_x(a, side):
    lane = lax.broadcasted_iota(jnp.int32, (8, 256), 1)
    out = jnp.zeros((8, 256), F32)
    for c in range(4):
        out = jnp.where(lane // 36 == c, roll_lane(a[c, 3 * side], 36 * (c - 5 * side)), out)
    return out


def pack_y(a, side):
    lane = lax.broadcasted_iota(jnp.int32, (8, 256), 1)
    sub = lax.broadcasted_iota(jnp.int32, (8, 256), 0)
    out = jnp.zeros((8, 256), F32)
    for c in range(4):
        rows = roll_sub(a[c, 0], -6 * side)
        for e in range(1, 4):
            rows = jnp.where(sub // 2 == e, roll_sub(a[c, e], 2 * e - 6 * side), rows)
        out = jnp.where((lane // 6) % 6 == c, roll_lane(rows, 6 * (c - 5 * side)), out)
    return out


def pack_z(a, side):
    lane = lax.broadcasted_iota(jnp.int32, (8, 256), 1)
    sub = lax.broadcasted_iota(jnp.int32, (8, 256), 0)
    halves_z = []
    for h in range(2):
        out = jnp.zeros((8, 256), F32)
        for c in range(4):
            even, odd = a[c, 2 * h], a[c, 2 * h + 1]
            rows = jnp.where(sub % 2 == 0, roll_sub(even, -side), roll_sub(odd, 1 - side))
            out = jnp.where(lane % 6 == c, roll_lane(rows, c - 5 * side), out)
        halves_z.append(out)
    return jnp.stack(halves_z, 0)


def turned(tile, sy, sz):
    lane = lax.broadcasted_iota(jnp.int32, (8, 256), 1)
    sub = lax.broadcasted_iota(jnp.int32, (8, 256), 0)
    here = None
    rows = lanes = 0
    if sy is not None:
        here = (sub // 2 == 3 * sy) & ((lane // 6) % 6 == 5 * sy)
        rows, lanes = 12 * sy - 6, 60 * sy - 30
    if sz is not None:
        also = (sub % 2 == sz) & (lane % 6 == 5 * sz)
        here = also if here is None else here & also
        rows, lanes = rows + 2 * sz - 1, lanes + 10 * sz - 5
    return jnp.where(here, roll_lane(roll_sub(tile, rows), lanes), 0.0)


def unpack_x(got, side):
    lane = lax.broadcasted_iota(jnp.int32, (8, 256), 1)
    face = lane // 36 == 5 * side
    parts = [jnp.where(face, roll_lane(got, 36 * (5 * side - c)), 0.0) for c in range(4)]
    return jnp.stack(parts, 0)


def unpack_y(got, side):
    lane = lax.broadcasted_iota(jnp.int32, (8, 256), 1)
    sub = lax.broadcasted_iota(jnp.int32, (8, 256), 0)
    face = (lane // 6) % 6 == 5 * side
    comps = []
    for c in range(4):
        rows = jnp.where(face, roll_lane(got, 6 * (5 * side - c)), 0.0)
        tiles = [
            jnp.where(sub // 2 == 3 * side, roll_sub(rows, 6 * side - 2 * e), 0.0) for e in range(4)
        ]
        comps.append(jnp.stack(tiles, 0))
    return jnp.stack(comps, 0)


def unpack_z(got, side):
    lane = lax.broadcasted_iota(jnp.int32, (8, 256), 1)
    sub = lax.broadcasted_iota(jnp.int32, (8, 256), 0)
    face = lane % 6 == 5 * side
    comps = []
    for c in range(4):
        tiles = []
        for e in range(4):
            rows = jnp.where(face, roll_lane(got[e // 2], 5 * side - c), 0.0)
            tiles.append(jnp.where(sub % 2 == side, roll_sub(rows, side - e % 2), 0.0))
        comps.append(jnp.stack(tiles, 0))
    return jnp.stack(comps, 0)


def whole_kernel(
    src_hbm, owner_hbm, local_hbm, jac_hbm, sh_hbm, sl_hbm, ph_hbm, pl_hbm, fh_hbm, fl_hbm,
    remapped_ref, accel_ref,
    src_v, a0, a1, a2, a3, a4, a5, a6, a7, b0, b1, b2, b3, b4, b5, b6, b7, send_a, send_b, arr_a, arr_b, rows_a, rows_b, rows_c,
    req_v, rreq_v, pos_v, req_s, pos_s,
    owner_v, local_v, jac_v, sh_v, sl_v, ph_v, pl_v, fh_v, fl_v,
    face_x, face_y, face_z, got_x, got_y, got_z, got_xy, got_xz, got_yz, got_xyz,
    ring_send, ring_recv, req_send, req_recv, row_send, row_recv, copy_sem, load_sem,
    face_send, face_recv,
):
    x = lax.axis_index("gx")
    z = lax.axis_index("gy")
    y = lax.axis_index("gz")
    right = lax.rem(z + 1, NY)
    left = lax.rem(z + NY - 1, NY)
    ahead = [lax.rem(x + i, NX) for i in range(NX)]
    place = (x, z, y)
    counts = (NX, NY, NZ)
    names = ("gx", "gy", "gz")
    blk_a = [a0, a1, a2, a3, a4, a5, a6, a7]
    blk_b = [b0, b1, b2, b3, b4, b5, b6, b7]
    blocks = (blk_a, blk_b)
    outgoing = (send_a, send_b)
    incoming = (arr_a, arr_b)

    def has(offset):
        ok = None
        for here, count, o in zip(place, counts, offset):
            if o:
                one = here < count - 1 if o > 0 else here > 0
                ok = one if ok is None else ok & one
        return ok

    def at(offset):
        return {
            name: jnp.clip(here + o, 0, count - 1)
            for name, here, count, o in zip(names, place, counts, offset)
            if o
        }

    small = [
        pltpu.make_async_copy(owner_hbm, owner_v, load_sem.at[8]),
        pltpu.make_async_copy(local_hbm, local_v, load_sem.at[9]),
    ]
    for one in small:
        one.start()
    own_load = pltpu.make_async_copy(src_hbm, src_v, load_sem.at[0])
    own_load.start()

    for ref in (got_x, got_y, got_z, got_xy, got_xz, got_yz, got_xyz):
        ref[...] = jnp.zeros_like(ref)

    barrier = pltpu.get_barrier_semaphore()
    for axis, where in (
        ("gy", left), ("gy", right), ("gx", ahead[1]), ("gx", ahead[2]), ("gx", ahead[3])
    ):
        pl.semaphore_signal(barrier, inc=1, device_id={axis: where}, device_id_type=MESH)
    near = 5
    for offset in OFFSETS:
        if offset[2] or (offset[0] and offset[1]):

            @pl.when(has(offset))
            def _():
                pl.semaphore_signal(barrier, inc=1, device_id=at(offset), device_id_type=MESH)

            near = near + jnp.where(has(offset), 1, 0)

    count = ELEMS * OVL
    for one in small:
        one.wait()
    owner = jnp.concatenate([owner_v[k] for k in range(OVL)], 1)
    wanted = jnp.concatenate([local_v[k : k + 1, :] for k in range(OVL)], 1).astype(F32)
    group = ((owner // NY - x + NX) & 3) * NY + ((z - (owner & 7) + NY) & 7)
    hits = jnp.where(group == lax.broadcasted_iota(jnp.int32, (NX * NY, count), 0), 1.0, 0.0)
    tri = lax.broadcasted_iota(jnp.int32, (count, count), 0) < lax.broadcasted_iota(
        jnp.int32, (count, count), 1
    )
    earlier = jnp.dot(
        hits.astype(BF16), jnp.where(tri, 1.0, 0.0).astype(BF16), preferred_element_type=F32
    )
    rank = jnp.sum(earlier * hits, 0, keepdims=True).astype(jnp.int32)
    slot = lax.broadcasted_iota(jnp.int32, (128, count), 0)
    placed = jnp.where(slot == rank, wanted, 0.0)
    req_v[...] = lax.dot_general(
        hits.astype(BF16), placed.astype(BF16), (((1,), (1,)), ((), ())), preferred_element_type=F32
    ).astype(jnp.int32)
    pos_v[...] = group * CAP + jnp.minimum(rank, CAP - 1)

    own_load.wait()
    a0[...] = src_v[:, :WA]
    b0[...] = jnp.concatenate([src_v[:, WA:], jnp.zeros((ELEMS, WA + WB - WIDTH), F32)], 1)

    pl.semaphore_wait(barrier, near)

    def ask(i):
        return pltpu.make_async_remote_copy(
            src_ref=req_v.at[pl.ds(8 * i, 8)],
            dst_ref=rreq_v.at[i - 1],
            send_sem=req_send.at[i - 1],
            recv_sem=req_recv.at[i - 1],
            device_id={"gx": ahead[i]},
            device_id_type=MESH,
        )

    for i in range(1, NX):
        ask(i).start()

    def hop(part, way, d):
        dst = (d + 1) % 8 if way == 0 else (d + 7) % 8
        rows = pl.ds(16 * way, 16) if dst == 4 else pl.ds(0, ELEMS)
        return pltpu.make_async_remote_copy(
            src_ref=blocks[part][d].at[rows],
            dst_ref=blocks[part][dst].at[rows],
            send_sem=ring_send.at[part, way, d],
            recv_sem=ring_recv.at[part, way, dst],
            device_id={"gy": right if way == 0 else left},
            device_id_type=MESH,
        )

    hops = []

    def go(part, way, d):
        one = hop(part, way, d)
        one.start()
        hops.append(one)

    def pass_on(part, j):
        for way, d in ((0, j), (1, 8 - j)):
            hop(part, way, (d + 7) % 8 if way == 0 else (d + 1) % 8).wait_recv()
            if j < 4:
                go(part, way, d)

    go(0, 0, 0)
    go(0, 1, 0)
    asked = [
        pltpu.make_async_copy(rreq_v.at[i - 1], req_s.at[i], copy_sem.at[i]) for i in range(1, NX)
    ]
    mine_first = pltpu.make_async_copy(req_v.at[pl.ds(0, 8)], req_s.at[0], copy_sem.at[0])
    mine_first.start()
    pos_copy = pltpu.make_async_copy(pos_v, pos_s, copy_sem.at[4])
    pos_copy.start()
    loads = [
        pltpu.make_async_copy(a, b, load_sem.at[1 + i])
        for i, (a, b) in enumerate(
            zip(
                (jac_hbm, sh_hbm, sl_hbm, ph_hbm, pl_hbm, fh_hbm, fl_hbm),
                (jac_v, sh_v, sl_v, ph_v, pl_v, fh_v, fl_v),
            )
        )
    ]
    for one in loads:
        one.start()
    mine_first.wait()
    pos_copy.wait()
    for i in range(1, NX):
        ask(i).wait_recv()
        asked[i - 1].start()
    go(1, 0, 0)
    go(1, 1, 0)
    for one in asked:
        one.wait()

    def reply(part, i, d):
        return pltpu.make_async_remote_copy(
            src_ref=outgoing[part].at[pl.ds(((i - 1) * 8 + d) * CAP, CAP)],
            dst_ref=incoming[part].at[pl.ds((i * 8 + d) * CAP, CAP)],
            send_sem=row_send.at[part, i - 1, d],
            recv_sem=row_recv.at[part, i - 1, d],
            device_id={"gx": ahead[NX - i]},
            device_id_type=MESH,
        )

    def answer(part, d):
        block = blocks[part][d]

        def one_slot(s, carry):
            for i in range(NX):
                row = block[pl.ds(req_s[i, d, s] & (ELEMS - 1), 1), :]
                if i == 0:
                    incoming[part][d * CAP + s] = row
                else:
                    outgoing[part][((i - 1) * 8 + d) * CAP + s] = row
            return carry

        lax.fori_loop(0, CAP, one_slot, 0)
        for i in (2, 1, 3):
            reply(part, i, d).start()

    def settle(part):
        for i in range(1, NX):
            for d in range(8):
                reply(part, i, d).wait_recv()

    answer(0, 0)
    for j in range(1, 5):
        pass_on(0, j)
        answer(0, j)
        if j < 4:
            answer(0, 8 - j)
        pass_on(1, j)
        for d in ((0,), (1, 7), (2, 6), (3, 5, 4))[j - 1]:
            answer(1, d)

    for one in loads:
        one.wait()

    def remap(part, extra):
        fields = (2, 3)[part]
        held = (rows_a, rows_b)[part]
        total = jnp.zeros(((fields + extra) * ELEMS, NB), F32)
        for k in range(OVL):
            buf = held.at[k % 2]
            for r in range(ELEMS):
                at = jnp.clip(pos_s[0, k * ELEMS + r], 0, SLOTS - 1)
                buf[pl.ds(r, 1), :] = incoming[part][at]
                if part == 1:
                    rows_c[k % 2, pl.ds(r, 1), :] = arr_a[at, :, WA - 128 :]
            rows = buf[...]
            if part == 1:
                rows = jnp.concatenate([rows_c[k % 2][:, 128 - TAIL :], rows[:, : 3 * NB - TAIL]], 1)
            lhs = jnp.concatenate([rows[:, f * NB : (f + 1) * NB] for f in range(fields)], 0)
            values = dot3(lhs, sh_v[k], sl_v[k])
            weight = jac_v[:, k * QP : (k + 1) * QP]
            scaled = [values[f * ELEMS : (f + 1) * ELEMS] * weight for f in range(fields)]
            total += dot3(jnp.concatenate(scaled + [weight] * extra, 0), ph_v[k], pl_v[k])
        return [total[f * ELEMS : (f + 1) * ELEMS] for f in range(fields + extra)]

    settle(0)
    first, second, lumped = remap(0, 1)
    first = first / lumped
    second = second / lumped
    force = dot3(first * second, fh_v[...], fl_v[...])
    mass = jnp.concatenate([lumped, jnp.zeros((ELEMS, 40), F32)], 1)
    a = jnp.stack([force[:, :256], force[:, 256:512], force[:, 512:], mass], 0)
    a = a.reshape(4, 4, 8, 256)

    for dim in range(3):
        a = shared_inside(dim, a)

    def face(n):
        offset = OFFSETS[n]
        sx, sy, sz = ((o + 1) // 2 for o in offset)
        if offset[0]:
            src = face_x.at[sx]
            if not offset[1] and not offset[2]:
                dst = got_x.at[1 - sx]
            elif not offset[1]:
                dst = got_xz.at[1 - sx, 1 - sz]
            elif not offset[2]:
                dst = got_xy.at[1 - sx, 1 - sy]
            else:
                dst = got_xyz.at[1 - sx, 1 - sy, 1 - sz]
        elif offset[1]:
            src = face_y.at[sy]
            dst = got_yz.at[1 - sy, 1 - sz] if offset[2] else got_y.at[1 - sy]
        else:
            src, dst = face_z.at[sz], got_z.at[1 - sz]
        return pltpu.make_async_remote_copy(
            src_ref=src,
            dst_ref=dst,
            send_sem=face_send.at[n],
            recv_sem=face_recv.at[n],
            device_id=at(offset),
            device_id_type=MESH,
        )

    def start_faces(which):
        for n in which:

            @pl.when(has(OFFSETS[n]))
            def _():
                face(n).start()

    for side in range(2):
        face_x[side] = pack_x(a, side)
    start_faces([n for n, o in enumerate(OFFSETS) if o[0]])
    for side in range(2):
        face_y[side] = pack_y(a, side)
    start_faces([n for n, o in enumerate(OFFSETS) if not o[0] and o[1]])
    for side in range(2):
        face_z[side] = pack_z(a, side)
    start_faces([n for n, o in enumerate(OFFSETS) if not o[0] and not o[1]])
    for n, offset in enumerate(OFFSETS):

        @pl.when(has(offset))
        def _():
            face(n).wait_send()

    for one in hops:
        one.wait_send()
    for i in range(1, NX):
        ask(i).wait_send()
        for d in range(8):
            reply(0, i, d).wait_send()

    settle(1)
    rest = [one / lumped for one in remap(1, 0)]
    remapped_ref[...] = jnp.concatenate([first, second] + rest, 1)

    for n, offset in enumerate(OFFSETS):

        @pl.when(has([-o for o in offset]))
        def _():
            face(n).wait_recv()

    gain_x = []
    gain_y = []
    for side in range(2):
        got = got_x[side]
        for one in range(2):
            got = got + turned(got_xy[side, one], one, None) + turned(got_xz[side, one], None, one)
            got = got + turned(got_xyz[side, 0, one], 0, one) + turned(got_xyz[side, 1, one], 1, one)
        gain_x.append(unpack_x(got, side))
        got = got_y[side]
        for one in range(2):
            got = got + turned(got_yz[side, one], None, one)
        gain_y.append(unpack_y(got, side))
    none = jnp.zeros_like(gain_x[0])
    a = a + jnp.stack([gain_x[0], none, none, gain_x[1]], 1) + gain_y[0] + gain_y[1]
    a = a + unpack_z(got_z[0], 0) + unpack_z(got_z[1], 1)
    mass = a[3].reshape(ELEMS, 256)[:, :NB]
    accel = [a[c].reshape(ELEMS, 256)[:, :NB] / mass for c in range(3)]
    accel_ref[...] = jnp.concatenate(accel, 1)

    for i in range(1, NX):
        for d in range(8):
            reply(1, i, d).wait_send()


def store_kernel(remapped_ref, accel_ref, remapped_hbm, accel_hbm, sem):
    copies = [
        pltpu.make_async_copy(remapped_ref, remapped_hbm, sem.at[0]),
        pltpu.make_async_copy(accel_ref, accel_hbm, sem.at[1]),
    ]
    for one in copies:
        one.start()
    for one in copies:
        one.wait()


def store(remapped, accel):
    vmem = pl.BlockSpec(memory_space=pltpu.VMEM)
    hbm = pl.BlockSpec(memory_space=pltpu.HBM)
    return pl.pallas_call(
        store_kernel,
        out_shape=(
            jax.ShapeDtypeStruct(remapped.shape, F32),
            jax.ShapeDtypeStruct(accel.shape, F32),
        ),
        in_specs=[vmem, vmem],
        out_specs=(hbm, hbm),
        scratch_shapes=[pltpu.SemaphoreType.DMA((2,))],
        compiler_params=pltpu.CompilerParams(vmem_limit_bytes=4 << 20),
        name="store",
    )(remapped, accel)


def per_device(src_fields, owner_peer, src_local, jac):
    source_tab, project_tab = remap_tables()
    tables = [*two_parts(source_tab), *two_parts(project_tab), *two_parts(force_table())]
    vmem = pl.BlockSpec(memory_space=pltpu.VMEM)
    hbm = pl.BlockSpec(memory_space=pltpu.HBM)
    dma = pltpu.SemaphoreType.DMA
    made = pl.pallas_call(
        whole_kernel,
        out_shape=(
            jax.ShapeDtypeStruct((ELEMS, WIDTH), F32),
            jax.ShapeDtypeStruct((ELEMS, 3 * NB), F32),
        ),
        in_specs=[hbm] * 10,
        out_specs=(vmem, vmem),
        scratch_shapes=[
            pltpu.VMEM((ELEMS, WIDTH), F32),
            *[pltpu.VMEM((ELEMS, WA), F32) for _ in range(NY)],
            *[pltpu.VMEM((ELEMS, WB), F32) for _ in range(NY)],
            pltpu.VMEM(((NX - 1) * NY * CAP, 1, WA), F32),
            pltpu.VMEM(((NX - 1) * NY * CAP, 1, WB), F32),
            pltpu.VMEM((SLOTS, 1, WA), F32),
            pltpu.VMEM((SLOTS, 1, WB), F32),
            pltpu.VMEM((2, ELEMS, WA), F32),
            pltpu.VMEM((2, ELEMS, WB), F32),
            pltpu.VMEM((2, ELEMS, 128), F32),
            pltpu.VMEM((NX * NY, 128), jnp.int32),
            pltpu.VMEM((NX - 1, NY, 128), jnp.int32),
            pltpu.VMEM((1, OVL * ELEMS), jnp.int32),
            pltpu.SMEM((NX, NY, 128), jnp.int32),
            pltpu.SMEM((1, OVL * ELEMS), jnp.int32),
            pltpu.VMEM((OVL, 1, ELEMS), jnp.int32),
            pltpu.VMEM((OVL, ELEMS), jnp.int32),
            pltpu.VMEM((ELEMS, OVL * QP), F32),
            pltpu.VMEM((OVL, NB, QP), BF16),
            pltpu.VMEM((OVL, NB, QP), BF16),
            pltpu.VMEM((OVL, QP, NB), BF16),
            pltpu.VMEM((OVL, QP, NB), BF16),
            pltpu.VMEM((NB, 768), BF16),
            pltpu.VMEM((NB, 768), BF16),
            pltpu.VMEM((2, 8, 256), F32),
            pltpu.VMEM((2, 8, 256), F32),
            pltpu.VMEM((2, 2, 8, 256), F32),
            pltpu.VMEM((2, 8, 256), F32),
            pltpu.VMEM((2, 8, 256), F32),
            pltpu.VMEM((2, 2, 8, 256), F32),
            pltpu.VMEM((2, 2, 8, 256), F32),
            pltpu.VMEM((2, 2, 8, 256), F32),
            pltpu.VMEM((2, 2, 8, 256), F32),
            pltpu.VMEM((2, 2, 2, 8, 256), F32),
            dma((2, 2, 8)),
            dma((2, 2, 8)),
            dma((NX - 1,)),
            dma((NX - 1,)),
            dma((2, NX - 1, NY)),
            dma((2, NX - 1, NY)),
            dma((5,)),
            dma((10,)),
            dma((26,)),
            dma((26,)),
        ],
        compiler_params=pltpu.CompilerParams(
            collective_id=0, has_side_effects=True, vmem_limit_bytes=30 << 20
        ),
        name="whole",
    )(
        pltpu.with_memory_space_constraint(src_fields, pltpu.HBM),
        pltpu.with_memory_space_constraint(jnp.transpose(owner_peer, (1, 2, 0)), pltpu.HBM),
        pltpu.with_memory_space_constraint(jnp.transpose(src_local, (1, 0)), pltpu.HBM),
        pltpu.with_memory_space_constraint(jac, pltpu.HBM),
        *[pltpu.with_memory_space_constraint(jnp.asarray(t), pltpu.HBM) for t in tables],
    )
    return store(*made)


def solution(mesh):
    placed = (
        P(("gx", "gy", "gz"), None),
        P(("gx", "gy", "gz"), None, None),
        P(("gx", "gy", "gz"), None),
        P(("gx", "gy", "gz"), None),
    )
    return jax.shard_map(
        per_device,
        mesh=mesh,
        in_specs=placed,
        out_specs=(P(("gx", "gy", "gz"), None), P(("gx", "gy", "gz"), None)),
        check_vma=False,
    )
```

```python
import math

import jax
import jax.numpy as jnp
import ml_dtypes
import numpy as np
from jax import lax
from jax.experimental import pallas as pl
from jax.experimental.pallas import tpu as pltpu
from jax.sharding import PartitionSpec as P

EX = 4
EY = 4
EZ = 2
FIELDS = 5
NB = 216
QP = 512
OVL = 8
ELEMS = 32
WIDTH = FIELDS * NB
WA = 512
WB = 640
TAIL = WA - 2 * NB
NX = 4
NY = 8
NZ = 8
CAP = 9
SLOTS = NX * NY * CAP
MESH = pl.DeviceIdType.MESH
OFFSETS = [
    (i, j, k) for i in (-1, 1, 0) for j in (-1, 1, 0) for k in (-1, 1, 0) if (i, j, k) != (0, 0, 0)
]
F32 = jnp.float32
BF16 = jnp.bfloat16


def bern_table(points):
    cols = [math.comb(5, i) * points**i * (1.0 - points) ** (5 - i) for i in range(6)]
    return np.stack(cols, -1)


def remap_tables():
    mids = (np.arange(8) + 0.5) / 16.0
    src_one = []
    tgt_one = []
    for bit in range(2):
        target_pts = bit * 0.5 + mids
        source_pts = target_pts + 0.5 - bit
        src_one.append(bern_table(source_pts).T)
        tgt_one.append(bern_table(target_pts) / 16.0)
    source_list = []
    project_list = []
    for intersection in range(8):
        bit_x, bit_y, bit_z = (intersection >> 2 & 1, intersection >> 1 & 1, intersection & 1)
        source_list.append(np.kron(src_one[bit_x], np.kron(src_one[bit_y], src_one[bit_z])))
        project_list.append(np.kron(tgt_one[bit_x], np.kron(tgt_one[bit_y], tgt_one[bit_z])))
    return np.stack(source_list), np.stack(project_list)


def lower_integral(first, second):
    if first < 0 or first > 4:
        return 0.0
    return math.comb(4, first) * math.comb(5, second) / (10.0 * math.comb(9, first + second))


def force_table():
    mass_one = np.zeros((6, 6))
    grad_one = np.zeros((6, 6))
    for left in range(6):
        for right in range(6):
            mass_one[left, right] = (
                math.comb(5, left) * math.comb(5, right) / (11.0 * math.comb(10, left + right))
            )
            grad_one[left, right] = 5.0 * (
                lower_integral(left - 1, right) - lower_integral(left, right)
            )
    grad_x = np.kron(grad_one, np.kron(mass_one, mass_one))
    grad_y = np.kron(mass_one, np.kron(grad_one, mass_one))
    grad_z = np.kron(mass_one, np.kron(mass_one, grad_one))
    padded = [np.pad(g.T * 8.0, ((0, 0), (0, 40))) for g in (grad_x, grad_y, grad_z)]
    return np.concatenate(padded, 1)


def two_parts(table):
    high = table.astype(ml_dtypes.bfloat16)
    low = (table - high.astype(np.float64)).astype(ml_dtypes.bfloat16)
    return high, low


def dot3(x, b_high, b_low):
    high = x.astype(BF16)
    low = (x - high.astype(F32)).astype(BF16)
    rows = x.shape[0]
    first = jnp.dot(jnp.concatenate([high, low], 0), b_high, preferred_element_type=F32)
    return first[:rows] + first[rows:] + jnp.dot(high, b_low, preferred_element_type=F32)


def roll_sub(v, by):
    return v if by % 8 == 0 else pltpu.roll(v, by % 8, len(v.shape) - 2)


def roll_lane(v, by):
    return v if by % 256 == 0 else pltpu.roll(v, by % 256, len(v.shape) - 1)


def shared_inside(dim, a):
    lane = lax.broadcasted_iota(jnp.int32, a.shape, 3)
    sub = lax.broadcasted_iota(jnp.int32, a.shape, 2)
    if dim == 0:
        edge = jnp.zeros_like(a[:, :1])
        up, down = jnp.concatenate([a[:, 1:], edge], 1), jnp.concatenate([edge, a[:, :3]], 1)
    elif dim == 1:
        up = jnp.where(sub // 2 == 3, 0.0, roll_sub(a, -2))
        down = jnp.where(sub // 2 == 0, 0.0, roll_sub(a, 2))
    else:
        up = jnp.where(sub % 2 == 1, 0.0, roll_sub(a, -1))
        down = jnp.where(sub % 2 == 0, 0.0, roll_sub(a, 1))
    step = (36, 6, 1)[dim]
    at = (lane // step) % 6
    gain = jnp.where(at == 5, roll_lane(up, 5 * step), 0.0)
    return a + gain + jnp.where(at == 0, roll_lane(down, -5 * step), 0.0)


def pack_x(a, side):
    lane = lax.broadcasted_iota(jnp.int32, (8, 256), 1)
    out = jnp.zeros((8, 256), F32)
    for c in range(4):
        out = jnp.where(lane // 36 == c, roll_lane(a[c, 3 * side], 36 * (c - 5 * side)), out)
    return out


def pack_y(a, side):
    lane = lax.broadcasted_iota(jnp.int32, (8, 256), 1)
    sub = lax.broadcasted_iota(jnp.int32, (8, 256), 0)
    out = jnp.zeros((8, 256), F32)
    for c in range(4):
        rows = roll_sub(a[c, 0], -6 * side)
        for e in range(1, 4):
            rows = jnp.where(sub // 2 == e, roll_sub(a[c, e], 2 * e - 6 * side), rows)
        out = jnp.where((lane // 6) % 6 == c, roll_lane(rows, 6 * (c - 5 * side)), out)
    return out


def pack_z(a, side):
    lane = lax.broadcasted_iota(jnp.int32, (8, 256), 1)
    sub = lax.broadcasted_iota(jnp.int32, (8, 256), 0)
    halves_z = []
    for h in range(2):
        out = jnp.zeros((8, 256), F32)
        for c in range(4):
            even, odd = a[c, 2 * h], a[c, 2 * h + 1]
            rows = jnp.where(sub % 2 == 0, roll_sub(even, -side), roll_sub(odd, 1 - side))
            out = jnp.where(lane % 6 == c, roll_lane(rows, c - 5 * side), out)
        halves_z.append(out)
    return jnp.stack(halves_z, 0)


def turned(tile, sy, sz):
    lane = lax.broadcasted_iota(jnp.int32, (8, 256), 1)
    sub = lax.broadcasted_iota(jnp.int32, (8, 256), 0)
    here = None
    rows = lanes = 0
    if sy is not None:
        here = (sub // 2 == 3 * sy) & ((lane // 6) % 6 == 5 * sy)
        rows, lanes = 12 * sy - 6, 60 * sy - 30
    if sz is not None:
        also = (sub % 2 == sz) & (lane % 6 == 5 * sz)
        here = also if here is None else here & also
        rows, lanes = rows + 2 * sz - 1, lanes + 10 * sz - 5
    return jnp.where(here, roll_lane(roll_sub(tile, rows), lanes), 0.0)


def unpack_x(got, side):
    lane = lax.broadcasted_iota(jnp.int32, (8, 256), 1)
    face = lane // 36 == 5 * side
    parts = [jnp.where(face, roll_lane(got, 36 * (5 * side - c)), 0.0) for c in range(4)]
    return jnp.stack(parts, 0)


def unpack_y(got, side):
    lane = lax.broadcasted_iota(jnp.int32, (8, 256), 1)
    sub = lax.broadcasted_iota(jnp.int32, (8, 256), 0)
    face = (lane // 6) % 6 == 5 * side
    comps = []
    for c in range(4):
        rows = jnp.where(face, roll_lane(got, 6 * (5 * side - c)), 0.0)
        tiles = [
            jnp.where(sub // 2 == 3 * side, roll_sub(rows, 6 * side - 2 * e), 0.0) for e in range(4)
        ]
        comps.append(jnp.stack(tiles, 0))
    return jnp.stack(comps, 0)


def unpack_z(got, side):
    lane = lax.broadcasted_iota(jnp.int32, (8, 256), 1)
    sub = lax.broadcasted_iota(jnp.int32, (8, 256), 0)
    face = lane % 6 == 5 * side
    comps = []
    for c in range(4):
        tiles = []
        for e in range(4):
            rows = jnp.where(face, roll_lane(got[e // 2], 5 * side - c), 0.0)
            tiles.append(jnp.where(sub % 2 == side, roll_sub(rows, side - e % 2), 0.0))
        comps.append(jnp.stack(tiles, 0))
    return jnp.stack(comps, 0)


def whole_kernel(
    src_hbm, owner_hbm, local_hbm, jac_hbm, sh_hbm, sl_hbm, ph_hbm, pl_hbm, fh_hbm, fl_hbm,
    remapped_ref, accel_ref,
    src_v, a0, a1, a2, a3, a4, a5, a6, a7, b0, b1, b2, b3, b4, b5, b6, b7, send_a, send_b, arr_a, arr_b, rows_a, rows_b,
    req_v, rreq_v, pos_v, req_s, pos_s,
    owner_v, local_v, jac_v, sh_v, sl_v, ph_v, pl_v, fh_v, fl_v,
    face_x, face_y, face_z, got_x, got_y, got_z, got_xy, got_xz, got_yz, got_xyz,
    ring_send, ring_recv, req_send, req_recv, row_send, row_recv, copy_sem, load_sem,
    face_send, face_recv,
):
    x = lax.axis_index("gx")
    z = lax.axis_index("gy")
    y = lax.axis_index("gz")
    right = lax.rem(z + 1, NY)
    left = lax.rem(z + NY - 1, NY)
    ahead = [lax.rem(x + i, NX) for i in range(NX)]
    place = (x, z, y)
    counts = (NX, NY, NZ)
    names = ("gx", "gy", "gz")
    blk_a = [a0, a1, a2, a3, a4, a5, a6, a7]
    blk_b = [b0, b1, b2, b3, b4, b5, b6, b7]
    blocks = (blk_a, blk_b)
    outgoing = (send_a, send_b)
    incoming = (arr_a, arr_b)

    def has(offset):
        ok = None
        for here, count, o in zip(place, counts, offset):
            if o:
                one = here < count - 1 if o > 0 else here > 0
                ok = one if ok is None else ok & one
        return ok

    def at(offset):
        return {
            name: jnp.clip(here + o, 0, count - 1)
            for name, here, count, o in zip(names, place, counts, offset)
            if o
        }

    small = [
        pltpu.make_async_copy(owner_hbm, owner_v, load_sem.at[8]),
        pltpu.make_async_copy(local_hbm, local_v, load_sem.at[9]),
    ]
    for one in small:
        one.start()
    own_load = pltpu.make_async_copy(src_hbm, src_v, load_sem.at[0])
    own_load.start()

    for ref in (got_x, got_y, got_z, got_xy, got_xz, got_yz, got_xyz):
        ref[...] = jnp.zeros_like(ref)

    barrier = pltpu.get_barrier_semaphore()
    for axis, where in (
        ("gy", left), ("gy", right), ("gx", ahead[1]), ("gx", ahead[2]), ("gx", ahead[3])
    ):
        pl.semaphore_signal(barrier, inc=1, device_id={axis: where}, device_id_type=MESH)
    near = 5
    for offset in OFFSETS:
        if offset[2] or (offset[0] and offset[1]):

            @pl.when(has(offset))
            def _():
                pl.semaphore_signal(barrier, inc=1, device_id=at(offset), device_id_type=MESH)

            near = near + jnp.where(has(offset), 1, 0)

    count = ELEMS * OVL
    for one in small:
        one.wait()
    owner = jnp.concatenate([owner_v[k] for k in range(OVL)], 1)
    wanted = jnp.concatenate([local_v[k : k + 1, :] for k in range(OVL)], 1).astype(F32)
    group = ((owner // NY - x + NX) & 3) * NY + ((z - (owner & 7) + NY) & 7)
    hits = jnp.where(group == lax.broadcasted_iota(jnp.int32, (NX * NY, count), 0), 1.0, 0.0)
    tri = lax.broadcasted_iota(jnp.int32, (count, count), 0) < lax.broadcasted_iota(
        jnp.int32, (count, count), 1
    )
    earlier = jnp.dot(
        hits.astype(BF16), jnp.where(tri, 1.0, 0.0).astype(BF16), preferred_element_type=F32
    )
    rank = jnp.sum(earlier * hits, 0, keepdims=True).astype(jnp.int32)
    slot = lax.broadcasted_iota(jnp.int32, (128, count), 0)
    placed = jnp.where(slot == rank, wanted, 0.0)
    req_v[...] = lax.dot_general(
        hits.astype(BF16), placed.astype(BF16), (((1,), (1,)), ((), ())), preferred_element_type=F32
    ).astype(jnp.int32)
    pos_v[...] = group * CAP + jnp.minimum(rank, CAP - 1)

    own_load.wait()
    a0[...] = src_v[:, :WA]
    b0[...] = jnp.concatenate([src_v[:, WA:], jnp.zeros((ELEMS, WA + WB - WIDTH), F32)], 1)

    pl.semaphore_wait(barrier, near)

    def ask(i):
        return pltpu.make_async_remote_copy(
            src_ref=req_v.at[pl.ds(8 * i, 8)],
            dst_ref=rreq_v.at[i - 1],
            send_sem=req_send.at[i - 1],
            recv_sem=req_recv.at[i - 1],
            device_id={"gx": ahead[i]},
            device_id_type=MESH,
        )

    for i in range(1, NX):
        ask(i).start()

    def hop(part, way, d):
        dst = (d + 1) % 8 if way == 0 else (d + 7) % 8
        rows = pl.ds(16 * way, 16) if dst == 4 else pl.ds(0, ELEMS)
        return pltpu.make_async_remote_copy(
            src_ref=blocks[part][d].at[rows],
            dst_ref=blocks[part][dst].at[rows],
            send_sem=ring_send.at[part, way, d],
            recv_sem=ring_recv.at[part, way, dst],
            device_id={"gy": right if way == 0 else left},
            device_id_type=MESH,
        )

    hops = []

    def go(part, way, d):
        one = hop(part, way, d)
        one.start()
        hops.append(one)

    def pass_on(part, j):
        for way, d in ((0, j), (1, 8 - j)):
            hop(part, way, (d + 7) % 8 if way == 0 else (d + 1) % 8).wait_recv()
            if j < 4:
                go(part, way, d)

    go(0, 0, 0)
    go(0, 1, 0)
    go(1, 0, 0)
    go(1, 1, 0)
    asked = [
        pltpu.make_async_copy(rreq_v.at[i - 1], req_s.at[i], copy_sem.at[i]) for i in range(1, NX)
    ]
    mine_first = pltpu.make_async_copy(req_v.at[pl.ds(0, 8)], req_s.at[0], copy_sem.at[0])
    mine_first.start()
    pos_copy = pltpu.make_async_copy(pos_v, pos_s, copy_sem.at[4])
    pos_copy.start()
    loads = [
        pltpu.make_async_copy(a, b, load_sem.at[1 + i])
        for i, (a, b) in enumerate(
            zip(
                (jac_hbm, sh_hbm, sl_hbm, ph_hbm, pl_hbm, fh_hbm, fl_hbm),
                (jac_v, sh_v, sl_v, ph_v, pl_v, fh_v, fl_v),
            )
        )
    ]
    for one in loads:
        one.start()
    mine_first.wait()
    pos_copy.wait()
    for i in range(1, NX):
        ask(i).wait_recv()
        asked[i - 1].start()
    for one in asked:
        one.wait()

    def reply(part, i, d):
        return pltpu.make_async_remote_copy(
            src_ref=outgoing[part].at[pl.ds(((i - 1) * 8 + d) * CAP, CAP)],
            dst_ref=incoming[part].at[pl.ds((i * 8 + d) * CAP, CAP)],
            send_sem=row_send.at[part, i - 1, d],
            recv_sem=row_recv.at[part, i - 1, d],
            device_id={"gx": ahead[NX - i]},
            device_id_type=MESH,
        )

    def answer(part, d):
        block = blocks[part][d]

        def one_slot(s, carry):
            for i in range(NX):
                row = block[pl.ds(req_s[i, d, s] & (ELEMS - 1), 1), :]
                if i == 0:
                    incoming[part][d * CAP + s] = row
                else:
                    outgoing[part][((i - 1) * 8 + d) * CAP + s] = row
            return carry

        lax.fori_loop(0, CAP, one_slot, 0)
        for i in (2, 1, 3):
            reply(part, i, d).start()

    def settle(part):
        for i in range(1, NX):
            for d in range(8):
                reply(part, i, d).wait_recv()

    answer(0, 0)
    for j in range(1, 5):
        pass_on(0, j)
        answer(0, j)
        if j < 4:
            answer(0, 8 - j)
        pass_on(1, j)
        for d in ((0, 1, 7), (2, 6), (3, 5), (4,))[j - 1]:
            answer(1, d)

    for one in loads:
        one.wait()

    def remap(part, extra):
        fields = (2, 3)[part]
        total = jnp.zeros(((fields + extra) * ELEMS, NB), F32)
        for k in range(OVL):
            buf = rows_b.at[k % 2] if part else rows_a.at[k]
            for r in range(ELEMS):
                at = jnp.clip(pos_s[0, k * ELEMS + r], 0, SLOTS - 1)
                buf[pl.ds(r, 1), :] = incoming[part][at]
            rows = buf[...]
            if part == 1:
                rows = jnp.concatenate([rows_a[k, :, 2 * NB :], rows[:, : 3 * NB - TAIL]], 1)
            lhs = jnp.concatenate([rows[:, f * NB : (f + 1) * NB] for f in range(fields)], 0)
            values = dot3(lhs, sh_v[k], sl_v[k])
            weight = jac_v[:, k * QP : (k + 1) * QP]
            scaled = [values[f * ELEMS : (f + 1) * ELEMS] * weight for f in range(fields)]
            total += dot3(jnp.concatenate(scaled + [weight] * extra, 0), ph_v[k], pl_v[k])
        return [total[f * ELEMS : (f + 1) * ELEMS] for f in range(fields + extra)]

    settle(0)
    first, second, lumped = remap(0, 1)
    first = first / lumped
    second = second / lumped
    force = dot3(first * second, fh_v[...], fl_v[...])
    mass = jnp.concatenate([lumped, jnp.zeros((ELEMS, 40), F32)], 1)
    a = jnp.stack([force[:, :256], force[:, 256:512], force[:, 512:], mass], 0)
    a = a.reshape(4, 4, 8, 256)

    for dim in range(3):
        a = shared_inside(dim, a)

    def face(n):
        offset = OFFSETS[n]
        sx, sy, sz = ((o + 1) // 2 for o in offset)
        if offset[0]:
            src = face_x.at[sx]
            if not offset[1] and not offset[2]:
                dst = got_x.at[1 - sx]
            elif not offset[1]:
                dst = got_xz.at[1 - sx, 1 - sz]
            elif not offset[2]:
                dst = got_xy.at[1 - sx, 1 - sy]
                src, dst = src.at[pl.ds(6 * sy, 2)], dst.at[pl.ds(6 * sy, 2)]
            else:
                dst = got_xyz.at[1 - sx, 1 - sy, 1 - sz]
                src, dst = src.at[pl.ds(6 * sy, 2)], dst.at[pl.ds(6 * sy, 2)]
        elif offset[1]:
            src = face_y.at[sy]
            dst = got_yz.at[1 - sy, 1 - sz] if offset[2] else got_y.at[1 - sy]
        else:
            src, dst = face_z.at[sz], got_z.at[1 - sz]
        return pltpu.make_async_remote_copy(
            src_ref=src,
            dst_ref=dst,
            send_sem=face_send.at[n],
            recv_sem=face_recv.at[n],
            device_id=at(offset),
            device_id_type=MESH,
        )

    def start_faces(which):
        for n in which:

            @pl.when(has(OFFSETS[n]))
            def _():
                face(n).start()

    for side in range(2):
        face_x[side] = pack_x(a, side)
    start_faces([n for n, o in enumerate(OFFSETS) if o[0]])
    for side in range(2):
        face_y[side] = pack_y(a, side)
    start_faces([n for n, o in enumerate(OFFSETS) if not o[0] and o[1]])
    for side in range(2):
        face_z[side] = pack_z(a, side)
    start_faces([n for n, o in enumerate(OFFSETS) if not o[0] and not o[1]])
    for n, offset in enumerate(OFFSETS):

        @pl.when(has(offset))
        def _():
            face(n).wait_send()

    for one in hops:
        one.wait_send()
    for i in range(1, NX):
        ask(i).wait_send()
        for d in range(8):
            reply(0, i, d).wait_send()

    settle(1)
    rest = [one / lumped for one in remap(1, 0)]
    remapped_ref[...] = jnp.concatenate([first, second] + rest, 1)

    for n, offset in enumerate(OFFSETS):

        @pl.when(has([-o for o in offset]))
        def _():
            face(n).wait_recv()

    gain_x = []
    gain_y = []
    for side in range(2):
        got = got_x[side]
        for one in range(2):
            got = got + turned(got_xy[side, one], one, None) + turned(got_xz[side, one], None, one)
            got = got + turned(got_xyz[side, 0, one], 0, one) + turned(got_xyz[side, 1, one], 1, one)
        gain_x.append(unpack_x(got, side))
        got = got_y[side]
        for one in range(2):
            got = got + turned(got_yz[side, one], None, one)
        gain_y.append(unpack_y(got, side))
    none = jnp.zeros_like(gain_x[0])
    a = a + jnp.stack([gain_x[0], none, none, gain_x[1]], 1) + gain_y[0] + gain_y[1]
    a = a + unpack_z(got_z[0], 0) + unpack_z(got_z[1], 1)
    mass = a[3].reshape(ELEMS, 256)[:, :NB]
    accel = [a[c].reshape(ELEMS, 256)[:, :NB] / mass for c in range(3)]
    accel_ref[...] = jnp.concatenate(accel, 1)

    for i in range(1, NX):
        for d in range(8):
            reply(1, i, d).wait_send()


def store_kernel(remapped_ref, accel_ref, remapped_hbm, accel_hbm, sem):
    copies = [
        pltpu.make_async_copy(remapped_ref, remapped_hbm, sem.at[0]),
        pltpu.make_async_copy(accel_ref, accel_hbm, sem.at[1]),
    ]
    for one in copies:
        one.start()
    for one in copies:
        one.wait()


def store(remapped, accel):
    vmem = pl.BlockSpec(memory_space=pltpu.VMEM)
    hbm = pl.BlockSpec(memory_space=pltpu.HBM)
    return pl.pallas_call(
        store_kernel,
        out_shape=(
            jax.ShapeDtypeStruct(remapped.shape, F32),
            jax.ShapeDtypeStruct(accel.shape, F32),
        ),
        in_specs=[vmem, vmem],
        out_specs=(hbm, hbm),
        scratch_shapes=[pltpu.SemaphoreType.DMA((2,))],
        compiler_params=pltpu.CompilerParams(vmem_limit_bytes=4 << 20),
        name="store",
    )(remapped, accel)


def per_device(src_fields, owner_peer, src_local, jac):
    source_tab, project_tab = remap_tables()
    tables = [*two_parts(source_tab), *two_parts(project_tab), *two_parts(force_table())]
    vmem = pl.BlockSpec(memory_space=pltpu.VMEM)
    hbm = pl.BlockSpec(memory_space=pltpu.HBM)
    dma = pltpu.SemaphoreType.DMA
    made = pl.pallas_call(
        whole_kernel,
        out_shape=(
            jax.ShapeDtypeStruct((ELEMS, WIDTH), F32),
            jax.ShapeDtypeStruct((ELEMS, 3 * NB), F32),
        ),
        in_specs=[hbm] * 10,
        out_specs=(vmem, vmem),
        scratch_shapes=[
            pltpu.VMEM((ELEMS, WIDTH), F32),
            *[pltpu.VMEM((ELEMS, WA), F32) for _ in range(NY)],
            *[pltpu.VMEM((ELEMS, WB), F32) for _ in range(NY)],
            pltpu.VMEM(((NX - 1) * NY * CAP, 1, WA), F32),
            pltpu.VMEM(((NX - 1) * NY * CAP, 1, WB), F32),
            pltpu.VMEM((SLOTS, 1, WA), F32),
            pltpu.VMEM((SLOTS, 1, WB), F32),
            pltpu.VMEM((OVL, ELEMS, WA), F32),
            pltpu.VMEM((2, ELEMS, WB), F32),
            pltpu.VMEM((NX * NY, 128), jnp.int32),
            pltpu.VMEM((NX - 1, NY, 128), jnp.int32),
            pltpu.VMEM((1, OVL * ELEMS), jnp.int32),
            pltpu.SMEM((NX, NY, 128), jnp.int32),
            pltpu.SMEM((1, OVL * ELEMS), jnp.int32),
            pltpu.VMEM((OVL, 1, ELEMS), jnp.int32),
            pltpu.VMEM((OVL, ELEMS), jnp.int32),
            pltpu.VMEM((ELEMS, OVL * QP), F32),
            pltpu.VMEM((OVL, NB, QP), BF16),
            pltpu.VMEM((OVL, NB, QP), BF16),
            pltpu.VMEM((OVL, QP, NB), BF16),
            pltpu.VMEM((OVL, QP, NB), BF16),
            pltpu.VMEM((NB, 768), BF16),
            pltpu.VMEM((NB, 768), BF16),
            pltpu.VMEM((2, 8, 256), F32),
            pltpu.VMEM((2, 8, 256), F32),
            pltpu.VMEM((2, 2, 8, 256), F32),
            pltpu.VMEM((2, 8, 256), F32),
            pltpu.VMEM((2, 8, 256), F32),
            pltpu.VMEM((2, 2, 8, 256), F32),
            pltpu.VMEM((2, 2, 8, 256), F32),
            pltpu.VMEM((2, 2, 8, 256), F32),
            pltpu.VMEM((2, 2, 8, 256), F32),
            pltpu.VMEM((2, 2, 2, 8, 256), F32),
            dma((2, 2, 8)),
            dma((2, 2, 8)),
            dma((NX - 1,)),
            dma((NX - 1,)),
            dma((2, NX - 1, NY)),
            dma((2, NX - 1, NY)),
            dma((5,)),
            dma((10,)),
            dma((26,)),
            dma((26,)),
        ],
        compiler_params=pltpu.CompilerParams(
            collective_id=0, has_side_effects=True, vmem_limit_bytes=30 << 20
        ),
        name="whole",
    )(
        pltpu.with_memory_space_constraint(src_fields, pltpu.HBM),
        pltpu.with_memory_space_constraint(jnp.transpose(owner_peer, (1, 2, 0)), pltpu.HBM),
        pltpu.with_memory_space_constraint(jnp.transpose(src_local, (1, 0)), pltpu.HBM),
        pltpu.with_memory_space_constraint(jac, pltpu.HBM),
        *[pltpu.with_memory_space_constraint(jnp.asarray(t), pltpu.HBM) for t in tables],
    )
    return store(*made)


def solution(mesh):
    placed = (
        P(("gx", "gy", "gz"), None),
        P(("gx", "gy", "gz"), None, None),
        P(("gx", "gy", "gz"), None),
        P(("gx", "gy", "gz"), None),
    )
    return jax.shard_map(
        per_device,
        mesh=mesh,
        in_specs=placed,
        out_specs=(P(("gx", "gy", "gz"), None), P(("gx", "gy", "gz"), None)),
        check_vma=False,
    )
```

```python
import math

import jax
import jax.numpy as jnp
import ml_dtypes
import numpy as np
from jax import lax
from jax.experimental import pallas as pl
from jax.experimental.pallas import tpu as pltpu
from jax.sharding import PartitionSpec as P

EX = 4
EY = 4
EZ = 2
FIELDS = 5
NB = 216
QP = 512
OVL = 8
ELEMS = 32
WIDTH = FIELDS * NB
WA = 512
WB = 640
TAIL = WA - 2 * NB
NX = 4
NY = 8
NZ = 8
CAP = 9
SLOTS = NX * NY * CAP
MESH = pl.DeviceIdType.MESH
OFFSETS = [
    (i, j, k) for i in (-1, 1, 0) for j in (-1, 1, 0) for k in (-1, 1, 0) if (i, j, k) != (0, 0, 0)
]
F32 = jnp.float32
BF16 = jnp.bfloat16


def bern_table(points):
    cols = [math.comb(5, i) * points**i * (1.0 - points) ** (5 - i) for i in range(6)]
    return np.stack(cols, -1)


def remap_tables():
    mids = (np.arange(8) + 0.5) / 16.0
    src_one = []
    tgt_one = []
    for bit in range(2):
        target_pts = bit * 0.5 + mids
        source_pts = target_pts + 0.5 - bit
        src_one.append(bern_table(source_pts).T)
        tgt_one.append(bern_table(target_pts) / 16.0)
    source_list = []
    project_list = []
    for intersection in range(8):
        bit_x, bit_y, bit_z = (intersection >> 2 & 1, intersection >> 1 & 1, intersection & 1)
        source_list.append(np.kron(src_one[bit_x], np.kron(src_one[bit_y], src_one[bit_z])))
        project_list.append(np.kron(tgt_one[bit_x], np.kron(tgt_one[bit_y], tgt_one[bit_z])))
    return np.stack(source_list), np.stack(project_list)


def lower_integral(first, second):
    if first < 0 or first > 4:
        return 0.0
    return math.comb(4, first) * math.comb(5, second) / (10.0 * math.comb(9, first + second))


def force_table():
    mass_one = np.zeros((6, 6))
    grad_one = np.zeros((6, 6))
    for left in range(6):
        for right in range(6):
            mass_one[left, right] = (
                math.comb(5, left) * math.comb(5, right) / (11.0 * math.comb(10, left + right))
            )
            grad_one[left, right] = 5.0 * (
                lower_integral(left - 1, right) - lower_integral(left, right)
            )
    grad_x = np.kron(grad_one, np.kron(mass_one, mass_one))
    grad_y = np.kron(mass_one, np.kron(grad_one, mass_one))
    grad_z = np.kron(mass_one, np.kron(mass_one, grad_one))
    padded = [np.pad(g.T * 8.0, ((0, 0), (0, 40))) for g in (grad_x, grad_y, grad_z)]
    return np.concatenate(padded, 1)


def two_parts(table):
    high = table.astype(ml_dtypes.bfloat16)
    low = (table - high.astype(np.float64)).astype(ml_dtypes.bfloat16)
    return high, low


def dot3(x, b_high, b_low):
    high = x.astype(BF16)
    low = (x - high.astype(F32)).astype(BF16)
    rows = x.shape[0]
    first = jnp.dot(jnp.concatenate([high, low], 0), b_high, preferred_element_type=F32)
    return first[:rows] + first[rows:] + jnp.dot(high, b_low, preferred_element_type=F32)


def roll_sub(v, by):
    return v if by % 8 == 0 else pltpu.roll(v, by % 8, len(v.shape) - 2)


def roll_lane(v, by):
    return v if by % 256 == 0 else pltpu.roll(v, by % 256, len(v.shape) - 1)


def shared_inside(dim, a):
    lane = lax.broadcasted_iota(jnp.int32, a.shape, 3)
    sub = lax.broadcasted_iota(jnp.int32, a.shape, 2)
    if dim == 0:
        edge = jnp.zeros_like(a[:, :1])
        up, down = jnp.concatenate([a[:, 1:], edge], 1), jnp.concatenate([edge, a[:, :3]], 1)
    elif dim == 1:
        up = jnp.where(sub // 2 == 3, 0.0, roll_sub(a, -2))
        down = jnp.where(sub // 2 == 0, 0.0, roll_sub(a, 2))
    else:
        up = jnp.where(sub % 2 == 1, 0.0, roll_sub(a, -1))
        down = jnp.where(sub % 2 == 0, 0.0, roll_sub(a, 1))
    step = (36, 6, 1)[dim]
    at = (lane // step) % 6
    gain = jnp.where(at == 5, roll_lane(up, 5 * step), 0.0)
    return a + gain + jnp.where(at == 0, roll_lane(down, -5 * step), 0.0)


def pack_x(a, side):
    lane = lax.broadcasted_iota(jnp.int32, (8, 256), 1)
    out = jnp.zeros((8, 256), F32)
    for c in range(4):
        out = jnp.where(lane // 36 == c, roll_lane(a[c, 3 * side], 36 * (c - 5 * side)), out)
    return out


def pack_y(a, side):
    lane = lax.broadcasted_iota(jnp.int32, (8, 256), 1)
    sub = lax.broadcasted_iota(jnp.int32, (8, 256), 0)
    out = jnp.zeros((8, 256), F32)
    for c in range(4):
        rows = roll_sub(a[c, 0], -6 * side)
        for e in range(1, 4):
            rows = jnp.where(sub // 2 == e, roll_sub(a[c, e], 2 * e - 6 * side), rows)
        out = jnp.where((lane // 6) % 6 == c, roll_lane(rows, 6 * (c - 5 * side)), out)
    return out


def pack_z(a, side):
    lane = lax.broadcasted_iota(jnp.int32, (8, 256), 1)
    sub = lax.broadcasted_iota(jnp.int32, (8, 256), 0)
    halves_z = []
    for h in range(2):
        out = jnp.zeros((8, 256), F32)
        for c in range(4):
            even, odd = a[c, 2 * h], a[c, 2 * h + 1]
            rows = jnp.where(sub % 2 == 0, roll_sub(even, -side), roll_sub(odd, 1 - side))
            out = jnp.where(lane % 6 == c, roll_lane(rows, c - 5 * side), out)
        halves_z.append(out)
    return jnp.stack(halves_z, 0)


def turned(tile, sy, sz):
    lane = lax.broadcasted_iota(jnp.int32, (8, 256), 1)
    sub = lax.broadcasted_iota(jnp.int32, (8, 256), 0)
    here = None
    rows = lanes = 0
    if sy is not None:
        here = (sub // 2 == 3 * sy) & ((lane // 6) % 6 == 5 * sy)
        rows, lanes = 12 * sy - 6, 60 * sy - 30
    if sz is not None:
        also = (sub % 2 == sz) & (lane % 6 == 5 * sz)
        here = also if here is None else here & also
        rows, lanes = rows + 2 * sz - 1, lanes + 10 * sz - 5
    return jnp.where(here, roll_lane(roll_sub(tile, rows), lanes), 0.0)


def unpack_x(got, side):
    lane = lax.broadcasted_iota(jnp.int32, (8, 256), 1)
    face = lane // 36 == 5 * side
    parts = [jnp.where(face, roll_lane(got, 36 * (5 * side - c)), 0.0) for c in range(4)]
    return jnp.stack(parts, 0)


def unpack_y(got, side):
    lane = lax.broadcasted_iota(jnp.int32, (8, 256), 1)
    sub = lax.broadcasted_iota(jnp.int32, (8, 256), 0)
    face = (lane // 6) % 6 == 5 * side
    comps = []
    for c in range(4):
        rows = jnp.where(face, roll_lane(got, 6 * (5 * side - c)), 0.0)
        tiles = [
            jnp.where(sub // 2 == 3 * side, roll_sub(rows, 6 * side - 2 * e), 0.0) for e in range(4)
        ]
        comps.append(jnp.stack(tiles, 0))
    return jnp.stack(comps, 0)


def unpack_z(got, side):
    lane = lax.broadcasted_iota(jnp.int32, (8, 256), 1)
    sub = lax.broadcasted_iota(jnp.int32, (8, 256), 0)
    face = lane % 6 == 5 * side
    comps = []
    for c in range(4):
        tiles = []
        for e in range(4):
            rows = jnp.where(face, roll_lane(got[e // 2], 5 * side - c), 0.0)
            tiles.append(jnp.where(sub % 2 == side, roll_sub(rows, side - e % 2), 0.0))
        comps.append(jnp.stack(tiles, 0))
    return jnp.stack(comps, 0)


def whole_kernel(
    src_hbm, owner_hbm, local_hbm, jac_hbm, sh_hbm, sl_hbm, ph_hbm, pl_hbm, fh_hbm, fl_hbm,
    remapped_ref, accel_ref,
    src_v, a0, a1, a2, a3, a4, a5, a6, a7, b0, b1, b2, b3, b4, b5, b6, b7, send_a, send_b, arr_a, arr_b, rows_a, rows_b,
    req_v, rreq_v, pos_v, req_s, pos_s,
    owner_v, local_v, jac_v, sh_v, sl_v, ph_v, pl_v, fh_v, fl_v,
    face_x, face_y, face_z, got_x, got_y, got_z, got_xy, got_xz, got_yz, got_xyz,
    ring_send, ring_recv, req_send, req_recv, row_send, row_recv, copy_sem, load_sem,
    face_send, face_recv,
):
    x = lax.axis_index("gx")
    z = lax.axis_index("gy")
    y = lax.axis_index("gz")
    right = lax.rem(z + 1, NY)
    left = lax.rem(z + NY - 1, NY)
    ahead = [lax.rem(x + i, NX) for i in range(NX)]
    place = (x, z, y)
    counts = (NX, NY, NZ)
    names = ("gx", "gy", "gz")
    blk_a = [a0, a1, a2, a3, a4, a5, a6, a7]
    blk_b = [b0, b1, b2, b3, b4, b5, b6, b7]
    blocks = (blk_a, blk_b)
    outgoing = (send_a, send_b)
    incoming = (arr_a, arr_b)

    def has(offset):
        ok = None
        for here, count, o in zip(place, counts, offset):
            if o:
                one = here < count - 1 if o > 0 else here > 0
                ok = one if ok is None else ok & one
        return ok

    def at(offset):
        return {
            name: jnp.clip(here + o, 0, count - 1)
            for name, here, count, o in zip(names, place, counts, offset)
            if o
        }

    small = [
        pltpu.make_async_copy(owner_hbm, owner_v, load_sem.at[8]),
        pltpu.make_async_copy(local_hbm, local_v, load_sem.at[9]),
    ]
    for one in small:
        one.start()
    own_load = pltpu.make_async_copy(src_hbm, src_v, load_sem.at[0])
    own_load.start()

    for ref in (got_x, got_y, got_z, got_xy, got_xz, got_yz, got_xyz):
        ref[...] = jnp.zeros_like(ref)

    barrier = pltpu.get_barrier_semaphore()
    for axis, where in (
        ("gy", left), ("gy", right), ("gx", ahead[1]), ("gx", ahead[2]), ("gx", ahead[3])
    ):
        pl.semaphore_signal(barrier, inc=1, device_id={axis: where}, device_id_type=MESH)
    near = 5
    for offset in OFFSETS:
        if offset[2] or (offset[0] and offset[1]):

            @pl.when(has(offset))
            def _():
                pl.semaphore_signal(barrier, inc=1, device_id=at(offset), device_id_type=MESH)

            near = near + jnp.where(has(offset), 1, 0)

    count = ELEMS * OVL
    for one in small:
        one.wait()
    owner = jnp.concatenate([owner_v[k] for k in range(OVL)], 1)
    wanted = jnp.concatenate([local_v[k : k + 1, :] for k in range(OVL)], 1).astype(F32)
    group = ((owner // NY - x + NX) & 3) * NY + ((z - (owner & 7) + NY) & 7)
    hits = jnp.where(group == lax.broadcasted_iota(jnp.int32, (NX * NY, count), 0), 1.0, 0.0)
    tri = lax.broadcasted_iota(jnp.int32, (count, count), 0) < lax.broadcasted_iota(
        jnp.int32, (count, count), 1
    )
    earlier = jnp.dot(
        hits.astype(BF16), jnp.where(tri, 1.0, 0.0).astype(BF16), preferred_element_type=F32
    )
    rank = jnp.sum(earlier * hits, 0, keepdims=True).astype(jnp.int32)
    slot = lax.broadcasted_iota(jnp.int32, (128, count), 0)
    placed = jnp.where(slot == rank, wanted, 0.0)
    req_v[...] = lax.dot_general(
        hits.astype(BF16), placed.astype(BF16), (((1,), (1,)), ((), ())), preferred_element_type=F32
    ).astype(jnp.int32)
    pos_v[...] = group * CAP + jnp.minimum(rank, CAP - 1)

    own_load.wait()
    a0[...] = src_v[:, :WA]
    b0[...] = jnp.concatenate([src_v[:, WA:], jnp.zeros((ELEMS, WA + WB - WIDTH), F32)], 1)

    pl.semaphore_wait(barrier, near)

    def ask(i):
        return pltpu.make_async_remote_copy(
            src_ref=req_v.at[pl.ds(8 * i, 8)],
            dst_ref=rreq_v.at[i - 1],
            send_sem=req_send.at[i - 1],
            recv_sem=req_recv.at[i - 1],
            device_id={"gx": ahead[i]},
            device_id_type=MESH,
        )

    for i in range(1, NX):
        ask(i).start()

    def hop(part, way, d):
        dst = (d + 1) % 8 if way == 0 else (d + 7) % 8
        rows = pl.ds(16 * way, 16) if dst == 4 else pl.ds(0, ELEMS)
        return pltpu.make_async_remote_copy(
            src_ref=blocks[part][d].at[rows],
            dst_ref=blocks[part][dst].at[rows],
            send_sem=ring_send.at[part, way, d],
            recv_sem=ring_recv.at[part, way, dst],
            device_id={"gy": right if way == 0 else left},
            device_id_type=MESH,
        )

    hops = []

    def go(part, way, d):
        one = hop(part, way, d)
        one.start()
        hops.append(one)

    def pass_on(part, j):
        for way, d in ((0, j), (1, 8 - j)):
            hop(part, way, (d + 7) % 8 if way == 0 else (d + 1) % 8).wait_recv()
            if j < 4:
                go(part, way, d)

    go(0, 0, 0)
    go(0, 1, 0)
    go(1, 0, 0)
    go(1, 1, 0)
    asked = [
        pltpu.make_async_copy(rreq_v.at[i - 1], req_s.at[i], copy_sem.at[i]) for i in range(1, NX)
    ]
    mine_first = pltpu.make_async_copy(req_v.at[pl.ds(0, 8)], req_s.at[0], copy_sem.at[0])
    mine_first.start()
    pos_copy = pltpu.make_async_copy(pos_v, pos_s, copy_sem.at[4])
    pos_copy.start()
    loads = [
        pltpu.make_async_copy(a, b, load_sem.at[1 + i])
        for i, (a, b) in enumerate(
            zip(
                (jac_hbm, sh_hbm, sl_hbm, ph_hbm, pl_hbm, fh_hbm, fl_hbm),
                (jac_v, sh_v, sl_v, ph_v, pl_v, fh_v, fl_v),
            )
        )
    ]
    for one in loads:
        one.start()
    mine_first.wait()
    pos_copy.wait()
    for i in range(1, NX):
        ask(i).wait_recv()
        asked[i - 1].start()
    for one in asked:
        one.wait()

    def reply(part, i, d):
        return pltpu.make_async_remote_copy(
            src_ref=outgoing[part].at[pl.ds(((i - 1) * 8 + d) * CAP, CAP)],
            dst_ref=incoming[part].at[pl.ds((i * 8 + d) * CAP, CAP)],
            send_sem=row_send.at[part, i - 1, d],
            recv_sem=row_recv.at[part, i - 1, d],
            device_id={"gx": ahead[NX - i]},
            device_id_type=MESH,
        )

    def answer(part, d):
        block = blocks[part][d]

        def one_slot(s, carry):
            for i in range(NX):
                row = block[pl.ds(req_s[i, d, s] & (ELEMS - 1), 1), :]
                if i == 0:
                    incoming[part][d * CAP + s] = row
                else:
                    outgoing[part][((i - 1) * 8 + d) * CAP + s] = row
            return carry

        lax.fori_loop(0, CAP, one_slot, 0)
        for i in (2, 1, 3):
            reply(part, i, d).start()

    def settle(part):
        for i in range(1, NX):
            for d in range(8):
                reply(part, i, d).wait_recv()

    answer(0, 0)
    answer(1, 0)
    for j in range(1, 5):
        pass_on(0, j)
        answer(0, j)
        if j < 4:
            answer(0, 8 - j)
        pass_on(1, j)
        for d in ((1, 7), (2, 6), (3, 5), (4,))[j - 1]:
            answer(1, d)

    for one in loads:
        one.wait()

    def remap(part, extra):
        fields = (2, 3)[part]
        total = jnp.zeros(((fields + extra) * ELEMS, NB), F32)
        for k in range(OVL):
            buf = rows_b.at[k % 2] if part else rows_a.at[k]
            for r in range(ELEMS):
                at = jnp.clip(pos_s[0, k * ELEMS + r], 0, SLOTS - 1)
                buf[pl.ds(r, 1), :] = incoming[part][at]
            rows = buf[...]
            if part == 1:
                rows = jnp.concatenate([rows_a[k, :, 2 * NB :], rows[:, : 3 * NB - TAIL]], 1)
            lhs = jnp.concatenate([rows[:, f * NB : (f + 1) * NB] for f in range(fields)], 0)
            values = dot3(lhs, sh_v[k], sl_v[k])
            weight = jac_v[:, k * QP : (k + 1) * QP]
            scaled = [values[f * ELEMS : (f + 1) * ELEMS] * weight for f in range(fields)]
            total += dot3(jnp.concatenate(scaled + [weight] * extra, 0), ph_v[k], pl_v[k])
        return [total[f * ELEMS : (f + 1) * ELEMS] for f in range(fields + extra)]

    settle(0)
    first, second, lumped = remap(0, 1)
    first = first / lumped
    second = second / lumped
    force = dot3(first * second, fh_v[...], fl_v[...])
    mass = jnp.concatenate([lumped, jnp.zeros((ELEMS, 40), F32)], 1)
    a = jnp.stack([force[:, :256], force[:, 256:512], force[:, 512:], mass], 0)
    a = a.reshape(4, 4, 8, 256)

    for dim in range(3):
        a = shared_inside(dim, a)

    def face(n):
        offset = OFFSETS[n]
        sx, sy, sz = ((o + 1) // 2 for o in offset)
        if offset[0]:
            src = face_x.at[sx]
            if not offset[1] and not offset[2]:
                dst = got_x.at[1 - sx]
            elif not offset[1]:
                dst = got_xz.at[1 - sx, 1 - sz]
            elif not offset[2]:
                dst = got_xy.at[1 - sx, 1 - sy]
                src, dst = src.at[pl.ds(6 * sy, 2)], dst.at[pl.ds(6 * sy, 2)]
            else:
                dst = got_xyz.at[1 - sx, 1 - sy, 1 - sz]
                src, dst = src.at[pl.ds(6 * sy, 2)], dst.at[pl.ds(6 * sy, 2)]
        elif offset[1]:
            src = face_y.at[sy]
            dst = got_yz.at[1 - sy, 1 - sz] if offset[2] else got_y.at[1 - sy]
        else:
            src, dst = face_z.at[sz], got_z.at[1 - sz]
        return pltpu.make_async_remote_copy(
            src_ref=src,
            dst_ref=dst,
            send_sem=face_send.at[n],
            recv_sem=face_recv.at[n],
            device_id=at(offset),
            device_id_type=MESH,
        )

    def start_faces(which):
        for n in which:

            @pl.when(has(OFFSETS[n]))
            def _():
                face(n).start()

    for side in range(2):
        face_x[side] = pack_x(a, side)
    start_faces([n for n, o in enumerate(OFFSETS) if o[0]])
    for side in range(2):
        face_y[side] = pack_y(a, side)
    start_faces([n for n, o in enumerate(OFFSETS) if not o[0] and o[1]])
    for side in range(2):
        face_z[side] = pack_z(a, side)
    start_faces([n for n, o in enumerate(OFFSETS) if not o[0] and not o[1]])
    for n, offset in enumerate(OFFSETS):

        @pl.when(has(offset))
        def _():
            face(n).wait_send()

    for one in hops:
        one.wait_send()
    for i in range(1, NX):
        ask(i).wait_send()
        for d in range(8):
            reply(0, i, d).wait_send()

    settle(1)
    rest = [one / lumped for one in remap(1, 0)]
    remapped_ref[...] = jnp.concatenate([first, second] + rest, 1)

    for n, offset in enumerate(OFFSETS):

        @pl.when(has([-o for o in offset]))
        def _():
            face(n).wait_recv()

    gain_x = []
    gain_y = []
    for side in range(2):
        got = got_x[side]
        for one in range(2):
            got = got + turned(got_xy[side, one], one, None) + turned(got_xz[side, one], None, one)
            got = got + turned(got_xyz[side, 0, one], 0, one) + turned(got_xyz[side, 1, one], 1, one)
        gain_x.append(unpack_x(got, side))
        got = got_y[side]
        for one in range(2):
            got = got + turned(got_yz[side, one], None, one)
        gain_y.append(unpack_y(got, side))
    none = jnp.zeros_like(gain_x[0])
    a = a + jnp.stack([gain_x[0], none, none, gain_x[1]], 1) + gain_y[0] + gain_y[1]
    a = a + unpack_z(got_z[0], 0) + unpack_z(got_z[1], 1)
    mass = a[3].reshape(ELEMS, 256)[:, :NB]
    accel = [a[c].reshape(ELEMS, 256)[:, :NB] / mass for c in range(3)]
    accel_ref[...] = jnp.concatenate(accel, 1)

    for i in range(1, NX):
        for d in range(8):
            reply(1, i, d).wait_send()


def store_kernel(remapped_ref, accel_ref, remapped_hbm, accel_hbm, sem):
    copies = [
        pltpu.make_async_copy(remapped_ref, remapped_hbm, sem.at[0]),
        pltpu.make_async_copy(accel_ref, accel_hbm, sem.at[1]),
    ]
    for one in copies:
        one.start()
    for one in copies:
        one.wait()


def store(remapped, accel):
    vmem = pl.BlockSpec(memory_space=pltpu.VMEM)
    hbm = pl.BlockSpec(memory_space=pltpu.HBM)
    return pl.pallas_call(
        store_kernel,
        out_shape=(
            jax.ShapeDtypeStruct(remapped.shape, F32),
            jax.ShapeDtypeStruct(accel.shape, F32),
        ),
        in_specs=[vmem, vmem],
        out_specs=(hbm, hbm),
        scratch_shapes=[pltpu.SemaphoreType.DMA((2,))],
        compiler_params=pltpu.CompilerParams(vmem_limit_bytes=4 << 20),
        name="store",
    )(remapped, accel)


def per_device(src_fields, owner_peer, src_local, jac):
    source_tab, project_tab = remap_tables()
    tables = [*two_parts(source_tab), *two_parts(project_tab), *two_parts(force_table())]
    vmem = pl.BlockSpec(memory_space=pltpu.VMEM)
    hbm = pl.BlockSpec(memory_space=pltpu.HBM)
    dma = pltpu.SemaphoreType.DMA
    made = pl.pallas_call(
        whole_kernel,
        out_shape=(
            jax.ShapeDtypeStruct((ELEMS, WIDTH), F32),
            jax.ShapeDtypeStruct((ELEMS, 3 * NB), F32),
        ),
        in_specs=[hbm] * 10,
        out_specs=(vmem, vmem),
        scratch_shapes=[
            pltpu.VMEM((ELEMS, WIDTH), F32),
            *[pltpu.VMEM((ELEMS, WA), F32) for _ in range(NY)],
            *[pltpu.VMEM((ELEMS, WB), F32) for _ in range(NY)],
            pltpu.VMEM(((NX - 1) * NY * CAP, 1, WA), F32),
            pltpu.VMEM(((NX - 1) * NY * CAP, 1, WB), F32),
            pltpu.VMEM((SLOTS, 1, WA), F32),
            pltpu.VMEM((SLOTS, 1, WB), F32),
            pltpu.VMEM((OVL, ELEMS, WA), F32),
            pltpu.VMEM((2, ELEMS, WB), F32),
            pltpu.VMEM((NX * NY, 128), jnp.int32),
            pltpu.VMEM((NX - 1, NY, 128), jnp.int32),
            pltpu.VMEM((1, OVL * ELEMS), jnp.int32),
            pltpu.SMEM((NX, NY, 128), jnp.int32),
            pltpu.SMEM((1, OVL * ELEMS), jnp.int32),
            pltpu.VMEM((OVL, 1, ELEMS), jnp.int32),
            pltpu.VMEM((OVL, ELEMS), jnp.int32),
            pltpu.VMEM((ELEMS, OVL * QP), F32),
            pltpu.VMEM((OVL, NB, QP), BF16),
            pltpu.VMEM((OVL, NB, QP), BF16),
            pltpu.VMEM((OVL, QP, NB), BF16),
            pltpu.VMEM((OVL, QP, NB), BF16),
            pltpu.VMEM((NB, 768), BF16),
            pltpu.VMEM((NB, 768), BF16),
            pltpu.VMEM((2, 8, 256), F32),
            pltpu.VMEM((2, 8, 256), F32),
            pltpu.VMEM((2, 2, 8, 256), F32),
            pltpu.VMEM((2, 8, 256), F32),
            pltpu.VMEM((2, 8, 256), F32),
            pltpu.VMEM((2, 2, 8, 256), F32),
            pltpu.VMEM((2, 2, 8, 256), F32),
            pltpu.VMEM((2, 2, 8, 256), F32),
            pltpu.VMEM((2, 2, 8, 256), F32),
            pltpu.VMEM((2, 2, 2, 8, 256), F32),
            dma((2, 2, 8)),
            dma((2, 2, 8)),
            dma((NX - 1,)),
            dma((NX - 1,)),
            dma((2, NX - 1, NY)),
            dma((2, NX - 1, NY)),
            dma((5,)),
            dma((10,)),
            dma((26,)),
            dma((26,)),
        ],
        compiler_params=pltpu.CompilerParams(
            collective_id=0, has_side_effects=True, vmem_limit_bytes=30 << 20
        ),
        name="whole",
    )(
        pltpu.with_memory_space_constraint(src_fields, pltpu.HBM),
        pltpu.with_memory_space_constraint(jnp.transpose(owner_peer, (1, 2, 0)), pltpu.HBM),
        pltpu.with_memory_space_constraint(jnp.transpose(src_local, (1, 0)), pltpu.HBM),
        pltpu.with_memory_space_constraint(jac, pltpu.HBM),
        *[pltpu.with_memory_space_constraint(jnp.asarray(t), pltpu.HBM) for t in tables],
    )
    return store(*made)


def solution(mesh):
    placed = (
        P(("gx", "gy", "gz"), None),
        P(("gx", "gy", "gz"), None, None),
        P(("gx", "gy", "gz"), None),
        P(("gx", "gy", "gz"), None),
    )
    return jax.shard_map(
        per_device,
        mesh=mesh,
        in_specs=placed,
        out_specs=(P(("gx", "gy", "gz"), None), P(("gx", "gy", "gz"), None)),
        check_vma=False,
    )
```
